32 devices in a mesh: dp: 8 (over z, core), ctx: 4 (over y, x).
Axes of the slice: x: 2, y: 2, z: 4, core: 2. Of those that a mesh axis runs over, the one named last changes fastest.
Arguments:
- inputs: bfloat16 [8, 1024, 1536], P('dp', 'ctx'), may hold values from -6 to 6
- cotangent: bfloat16 [8, 1024, 1536], P('dp', 'ctx'), may hold values from -6 to 6
- segment_ids: int32 [8, 1024], P('dp', 'ctx'), may hold values from 0 to 3, never falling along the last dimension, each value on 1 to 512 neighbouring positions
- attn_gain: bfloat16 [1536], P(('dp', 'ctx')), may hold values from 0.5 to 1.5
- qkv_weight: bfloat16 [1536, 2048], P(('dp', 'ctx')), may hold values from -0.15625 to 0.15625
- qkv_bias: bfloat16 [2048], P(('dp', 'ctx')), may hold values from -4 to 4
- out_weight: bfloat16 [1536, 1536], P(('dp', 'ctx')), may hold values from -0.875 to 0.875
- mlp_gain: bfloat16 [1536], P(('dp', 'ctx')), may hold values from 0.5 to 1.5
- gate_weight: bfloat16 [1536, 8960], P(('dp', 'ctx')), may hold values from -0.15625 to 0.15625
- up_weight: bfloat16 [1536, 8960], P(('dp', 'ctx')), may hold values from -0.15625 to 0.15625
- down_weight: bfloat16 [8960, 1536], P(('dp', 'ctx')), may hold values from -0.0625 to 0.0625
Outputs:
- output: bfloat16 [8, 1024, 1536], P('dp', 'ctx')
- input_grad: float32 [8, 1024, 1536], P('dp', 'ctx')
- attn_gain_grad: float32 [1536], P(('dp', 'ctx'))
- qkv_weight_grad: float32 [1536, 2048], P(('dp', 'ctx'))
- qkv_bias_grad: float32 [2048], P(('dp', 'ctx'))
- out_weight_grad: float32 [1536, 1536], P(('dp', 'ctx'))
- mlp_gain_grad: float32 [1536], P(('dp', 'ctx'))
- gate_weight_grad: float32 [1536, 8960], P(('dp', 'ctx'))
- up_weight_grad: float32 [1536, 8960], P(('dp', 'ctx'))
- down_weight_grad: float32 [8960, 1536], P(('dp', 'ctx'))
The draws below stay inside these ranges and needn't reach their ends.
Inputs may be any that keep to these rules, and one draw needn't show every extreme that they name: `segment_ids`: segment ids never fall along a sequence; each of the 4 documents of a sequence holds 1 to 512 tokens, and one holds exactly 512.
All inputs are finite; a program needn't handle non-finite values.
Results may differ from the reference program's by a relative error of at most 0.029.
The reference program's roundings to bfloat16 on the way count: a program that leaves them out, or rounds other values in their place, can miss the bound.
Values may be sent and summed in bfloat16 or wider, within the bound.
No kernel may reach another device: no remote copies, remote signals or barrier semaphores. Data moves between devices by JAX's collectives and lax.ppermute only.
A program may use at most 640 MiB of HBM per device.

```python
import math
import jax
import jax.numpy as jnp
import numpy as np
from jax import lax

D = 1536
H = 12
KV = 2
HD = 128
FF = 8960
DOCS = 4
LENGTH = 1024
SEQS = 8
QKV = 2048


def draw_qkv_bias(key, part):
    key_rest = jax.random.fold_in(key, 2)
    drawn = jnp.clip(jax.random.normal(key_rest, (QKV,), jnp.float32) * 0.5, -3.0, 3.0)
    return drawn.astype(jnp.bfloat16)


def shard_levels(key, dims, cuts, smallest, largest):
    level, own = 1.0, jax.random.fold_in(key, 6)
    for dim, shards_of in cuts:
        heights = jnp.exp(jax.random.uniform(jax.random.fold_in(own, dim), (shards_of,), jnp.float32, smallest / len(cuts), largest / len(cuts)))
        level = level * jnp.repeat(heights, dims[dim] // shards_of).reshape([-1 if axis == dim else 1 for axis in range(len(dims))])
    return level


def length_profile(count, total, limit, skew):
    loads = [(1 << 20) // math.isqrt(standing ** skew) + 1 for standing in range(2, count + 1)]
    spare, counts = total - limit - (count - 1), [1] * (count - 1)
    while spare > 0:
        free = [i for i in range(count - 1) if counts[i] < limit]
        whole, remaining = sum([loads[i] for i in free]), spare
        for i in free:
            addition = min(limit - counts[i], max(1, remaining * loads[i] // whole), spare)
            counts[i] = counts[i] + addition
            spare = spare - addition
    return np.array([limit] + counts)


def ragged(key, amount, total, limit, skew):
    if amount == 2:
        one = jax.random.randint(key, (), max(1, total - limit), min(limit, total - 1) + 1)
        return jnp.stack([one, total - one])
    tallies = jnp.asarray(length_profile(amount, total, limit, skew), jnp.int32)
    pairs = (amount - 1) // 2
    giver, taker = tallies[1:1 + 2 * pairs:2], tallies[2:2 + 2 * pairs:2]
    margin = jnp.minimum(giver - 1, limit - taker)
    passed = jax.random.randint(jax.random.fold_in(key, 1), (pairs,), 0, 1 << 20) % (margin + 1)
    tallies = tallies.at[1:1 + 2 * pairs:2].set(giver - passed).at[2:2 + 2 * pairs:2].set(taker + passed)
    return tallies[jax.random.permutation(jax.random.fold_in(key, 2), amount)]


def noise(own_key, extent, deviation, most, shards=(), kind=jnp.bfloat16):
    level = shard_levels(own_key, extent, shards, -0.22, 0.18) if shards else 1.0
    result = jax.random.normal(own_key, extent, jnp.float32) * deviation * level
    return jnp.minimum(jnp.maximum(result, -most), most).astype(kind)


def setup_inputs(seed: int = 0) -> dict:
    streams_of = jax.random.split(jax.random.key(seed), 12)
    return {
        "inputs": noise(streams_of[0], (SEQS, LENGTH, D), 1.0, 6.0, ((0, 8), (1, 4))),
        "cotangent": noise(streams_of[1], (SEQS, LENGTH, D), 1.0, 6.0, ((0, 8), (1, 4))),
        "segment_ids": jax.vmap(lambda own: jnp.searchsorted(jnp.cumsum(ragged(own, DOCS, LENGTH, LENGTH // 2, 1)), jnp.arange(LENGTH), side="right"))(jax.random.split(streams_of[2], SEQS)).reshape((SEQS, LENGTH)).astype(jnp.int32),
        "attn_gain": jnp.clip(1.0 + 0.1 * jax.random.normal(streams_of[3], (D,), jnp.float32), 0.5, 1.5).astype(jnp.bfloat16),
        "qkv_weight": noise(streams_of[4], (D, QKV), D ** -0.5, 0.15625, ((0, 32),)),
        "qkv_bias": draw_qkv_bias(jax.random.fold_in(streams_of[11], 71), 0),
        "out_weight": noise(streams_of[6], (H * HD, D), (H * HD // 32) ** -0.5, 0.875, ((0, 32),)),
        "mlp_gain": jnp.clip(1.0 + 0.1 * jax.random.normal(streams_of[7], (D,), jnp.float32), 0.5, 1.5).astype(jnp.bfloat16),
        "gate_weight": noise(streams_of[8], (D, FF), D ** -0.5, 0.15625, ((0, 32),)),
        "up_weight": noise(streams_of[9], (D, FF), D ** -0.5, 0.15625, ((0, 32),)),
        "down_weight": noise(streams_of[10], (FF, D), FF ** -0.5, 0.0625, ((0, 32),)),
    }


EPS = 1e-06
THETA = 1000000.0
MASKED = -1e+30

def rope_tables(positions):
    half_dim = jnp.arange(0, HD, 2).astype(jnp.float32) / HD
    inverse = THETA ** (-half_dim)
    angles = positions.astype(jnp.float32)[:, None] * inverse[None, :]
    angles = jnp.concatenate([angles, angles], axis=1)
    return (jnp.cos(angles), jnp.sin(angles))

def rotate(values, cos_table, sin_table):
    half_dim = values.shape[-1] // 2
    turned = jnp.concatenate([-values[..., half_dim:], values[..., :half_dim]], axis=-1)
    return values * cos_table[:, None, :] + turned * sin_table[:, None, :]

def rms_norm(values, gain):
    inv_rms = lax.rsqrt(lax.optimization_barrier(jnp.mean(values * values, axis=-1, keepdims=True)) + EPS)
    return (values * inv_rms * gain.astype(jnp.float32), inv_rms)

def norm_back(normed_grad, values, inv_rms, gain):
    normed = values * inv_rms
    gain_grad = lax.optimization_barrier(jnp.sum(normed_grad * normed, axis=0))
    scaled_grad = normed_grad * gain.astype(jnp.float32)
    values_grad = inv_rms * (scaled_grad - normed * lax.optimization_barrier(jnp.mean(scaled_grad * normed, axis=-1, keepdims=True)))
    return (values_grad, gain_grad)

def attend(queries, key_rows, value_rows, visible, scale_factor):
    per_group = queries.shape[1] // KV
    pieces = []
    totals = []
    for kv_group in range(KV):
        query_part = queries[:, kv_group * per_group:(kv_group + 1) * per_group, :].astype(jnp.float32)
        scores = jnp.einsum('tjd,nd->jtn', query_part, key_rows[:, kv_group, :].astype(jnp.float32)) * scale_factor
        scores = jnp.where(visible[None], scores, MASKED)
        row_max = lax.optimization_barrier(jnp.max(scores, axis=-1, keepdims=True))
        row_sum = lax.optimization_barrier(jnp.sum(jnp.exp(scores - row_max), axis=-1, keepdims=True))
        log_total = row_max + jnp.log(row_sum)
        weights = jnp.exp(scores - log_total).astype(jnp.bfloat16)
        mixed_part = jnp.einsum('jtn,nd->tjd', weights.astype(jnp.float32), value_rows[:, kv_group, :].astype(jnp.float32))
        pieces.append(mixed_part)
        totals.append(log_total)
    attended = jnp.concatenate(pieces, axis=1).astype(jnp.bfloat16)
    return (attended.reshape(queries.shape[0], -1), jnp.stack(totals))

def attend_back(queries, key_rows, value_rows, visible, attended, attended_grad, log_totals, scale_factor):
    tokens = queries.shape[0]
    per_group = queries.shape[1] // KV
    attended_heads = attended.reshape(tokens, H, HD)
    grad_heads = attended_grad.reshape(tokens, H, HD)
    query_grads = []
    key_grads = []
    value_grads = []
    for kv_group in range(KV):
        part = slice(kv_group * per_group, (kv_group + 1) * per_group)
        query_part = queries[:, part, :].astype(jnp.float32)
        out_part = attended_heads[:, part, :].astype(jnp.float32)
        grad_part = grad_heads[:, part, :].astype(jnp.float32)
        key_part = key_rows[:, kv_group, :].astype(jnp.float32)
        value_part = value_rows[:, kv_group, :].astype(jnp.float32)
        scores = jnp.einsum('tjd,nd->jtn', query_part, key_part) * scale_factor
        scores = jnp.where(visible[None], scores, MASKED)
        probs_full = jnp.exp(scores - log_totals[kv_group])
        probs_low = probs_full.astype(jnp.bfloat16).astype(jnp.float32)
        value_grads.append(jnp.einsum('jtn,tjd->nd', probs_low, grad_part))
        prob_grad = jnp.einsum('tjd,nd->jtn', grad_part, value_part)
        row_dot = lax.optimization_barrier(jnp.sum(grad_part * out_part, axis=-1)).T
        score_grad = (probs_full * (prob_grad - row_dot[..., None]) * scale_factor).astype(jnp.bfloat16).astype(jnp.float32)
        query_grads.append(jnp.einsum('jtn,nd->tjd', score_grad, key_part))
        key_grads.append(jnp.einsum('jtn,tjd->nd', score_grad, query_part))
    return (jnp.concatenate(query_grads, axis=1), jnp.stack(key_grads, axis=1), jnp.stack(value_grads, axis=1))

def layer_sequence(inputs, cotangent, segments, params):
    gain_one, full_qkv, bias_full, full_out, gain_two, full_gate, full_up, full_down = params
    length = inputs.shape[0]
    query_width = H * HD
    kv_width = KV * HD
    scale_factor = 1.0 / HD ** 0.5
    token_index = jnp.arange(length, dtype=jnp.int32)
    doc_start = lax.optimization_barrier(jnp.sum((segments[None, :] < segments[:, None]).astype(jnp.int32), axis=1))
    positions = token_index - doc_start
    visible = (token_index[None, :] <= token_index[:, None]) & (segments[None, :] == segments[:, None])
    cos_table, sin_table = rope_tables(positions)
    resid_in = inputs.astype(jnp.float32)
    normed_one, inv_one = rms_norm(resid_in, gain_one)
    normed_low = normed_one.astype(jnp.bfloat16)
    projected = jnp.dot(normed_low, full_qkv, preferred_element_type=jnp.float32) + bias_full.astype(jnp.float32)
    query_pre = projected[:, :query_width].reshape(length, H, HD)
    key_pre = projected[:, query_width:query_width + kv_width].reshape(length, KV, HD)
    value_rows = projected[:, query_width + kv_width:].astype(jnp.bfloat16).reshape(length, KV, HD)
    query_rot = rotate(query_pre, cos_table, sin_table).astype(jnp.bfloat16)
    key_rot = rotate(key_pre, cos_table, sin_table).astype(jnp.bfloat16)
    attended, log_totals = attend(query_rot, key_rot, value_rows, visible, scale_factor)
    resid_mid = resid_in + jnp.dot(attended, full_out, preferred_element_type=jnp.float32)
    normed_two, inv_two = rms_norm(resid_mid, gain_two)
    normed_two_low = normed_two.astype(jnp.bfloat16)
    gate_pre = jnp.dot(normed_two_low, full_gate, preferred_element_type=jnp.float32)
    up_pre = jnp.dot(normed_two_low, full_up, preferred_element_type=jnp.float32)
    sigmoid_gate = jax.nn.sigmoid(gate_pre)
    silu_gate = gate_pre * sigmoid_gate
    hidden = (silu_gate * up_pre).astype(jnp.bfloat16)
    output = (resid_mid + jnp.dot(hidden, full_down, preferred_element_type=jnp.float32)).astype(jnp.bfloat16)
    down_term = jnp.dot(hidden.T, cotangent, preferred_element_type=jnp.float32)
    hidden_grad = jnp.dot(cotangent, full_down.T, preferred_element_type=jnp.float32)
    gate_grad = (hidden_grad * up_pre * sigmoid_gate * (1.0 + gate_pre * (1.0 - sigmoid_gate))).astype(jnp.bfloat16)
    up_grad = (hidden_grad * silu_gate).astype(jnp.bfloat16)
    gate_term = jnp.dot(normed_two_low.T, gate_grad, preferred_element_type=jnp.float32)
    up_term = jnp.dot(normed_two_low.T, up_grad, preferred_element_type=jnp.float32)
    normed_two_grad = jnp.dot(gate_grad, full_gate.T, preferred_element_type=jnp.float32) + jnp.dot(up_grad, full_up.T, preferred_element_type=jnp.float32)
    mid_norm_grad, gain_two_term = norm_back(normed_two_grad, resid_mid, inv_two, gain_two)
    mid_grad = cotangent.astype(jnp.float32) + mid_norm_grad
    mid_grad_low = mid_grad.astype(jnp.bfloat16)
    out_term = jnp.dot(attended.T, mid_grad_low, preferred_element_type=jnp.float32)
    attended_grad = jnp.dot(mid_grad_low, full_out.T, preferred_element_type=jnp.float32).astype(jnp.bfloat16)
    query_grad, key_grad, value_grad = attend_back(query_rot, key_rot, value_rows, visible, attended, attended_grad, log_totals, scale_factor)
    query_grad_pre = rotate(query_grad, cos_table, -sin_table).reshape(length, query_width)
    key_grad_pre = rotate(key_grad, cos_table, -sin_table).reshape(length, kv_width)
    proj_grad = jnp.concatenate([query_grad_pre, key_grad_pre, value_grad.reshape(length, kv_width)], axis=1)
    bias_term = lax.optimization_barrier(jnp.sum(proj_grad, axis=0))
    proj_grad_low = proj_grad.astype(jnp.bfloat16)
    qkv_term = jnp.dot(normed_low.T, proj_grad_low, preferred_element_type=jnp.float32)
    normed_one_grad = jnp.dot(proj_grad_low, full_qkv.T, preferred_element_type=jnp.float32)
    in_norm_grad, gain_one_term = norm_back(normed_one_grad, resid_in, inv_one, gain_one)
    input_grad = mid_grad + in_norm_grad
    grads = (gain_one_term, qkv_term, bias_term, out_term, gain_two_term, gate_term, up_term, down_term)
    return (output, input_grad, grads)

def reference(inputs, cotangent, segment_ids, attn_gain, qkv_weight, qkv_bias, out_weight, mlp_gain, gate_weight, up_weight, down_weight):
    params = (attn_gain, qkv_weight, qkv_bias, out_weight, mlp_gain, gate_weight, up_weight, down_weight)
    zero_grads = tuple((jnp.zeros(weight.shape, jnp.float32) for weight in params))

    def add_sequence(running, sequence):
        output, input_grad, grads = layer_sequence(sequence[0], sequence[1], sequence[2], params)
        return (tuple((summed + added for summed, added in zip(running, grads))), (output, input_grad))
    totals, stacked = lax.scan(add_sequence, zero_grads, (inputs, cotangent, segment_ids))
    return (stacked[0], stacked[1], totals[0], totals[1], totals[2], totals[3], totals[4], totals[5], totals[6], totals[7])
```

```python
import functools
import math

import jax
import jax.numpy as jnp
from jax import lax
from jax.sharding import PartitionSpec as P

H = 12
KV = 2
HD = 128
LANES = 128


EPS = 1e-06
THETA = 1000000.0
MASKED = -1e30
BF = jnp.bfloat16
F32 = jnp.float32
DP = ("far", "near")
ALL = ("far", "near", "ctx")


def rope_tables(positions):
    half_dim = jnp.arange(0, HD, 2).astype(F32) / HD
    inverse = THETA ** (-half_dim)
    angles = positions.astype(F32)[:, None] * inverse[None, :]
    angles = jnp.concatenate([angles, angles], axis=1)
    return (jnp.cos(angles), jnp.sin(angles))


def rotate(values, cos_table, sin_table):
    half_dim = values.shape[-1] // 2
    turned = jnp.concatenate([-values[..., half_dim:], values[..., :half_dim]], axis=-1)
    return values * cos_table[:, None, :] + turned * sin_table[:, None, :]


def inv_rms_of(values):
    return lax.rsqrt(jnp.mean(values * values, axis=-1, keepdims=True) + EPS)


def norm_back(normed_grad, values, inv_rms, gain):
    normed = values * inv_rms
    scaled_grad = normed_grad * gain
    return inv_rms * (scaled_grad - normed * jnp.mean(scaled_grad * normed, axis=-1, keepdims=True))


def dot(a, b):
    return jnp.dot(a, b, preferred_element_type=F32)


def dot_t(a, b):
    return lax.dot_general(a, b, (((1,), (1,)), ((), ())), preferred_element_type=F32)


def t_dot(a, b):
    return lax.dot_general(a, b, (((0,), (0,)), ((), ())), preferred_element_type=F32)


def attend(queries, key_rows, value_rows, visible, scale_factor):
    scores = jnp.einsum("tjd,nd->jtn", queries, key_rows, preferred_element_type=F32) * scale_factor
    scores = jnp.where(visible[None], scores, MASKED)
    row_max = jnp.max(scores, axis=-1, keepdims=True)
    row_sum = jnp.sum(jnp.exp(scores - row_max), axis=-1, keepdims=True)
    log_total = row_max + jnp.log(row_sum)
    weights = jnp.exp(scores - log_total).astype(BF)
    mixed = jnp.einsum("jtn,nd->tjd", weights, value_rows, preferred_element_type=F32)
    return mixed, log_total


def attend_back(
    queries, key_rows, value_rows, visible, attended, attended_grad, log_total, scale_factor
):
    scores = jnp.einsum("tjd,nd->jtn", queries, key_rows, preferred_element_type=F32) * scale_factor
    scores = jnp.where(visible[None], scores, MASKED)
    probs_full = jnp.exp(scores - log_total)
    probs_low = probs_full.astype(BF)
    value_grad = jnp.einsum("jtn,tjd->nd", probs_low, attended_grad, preferred_element_type=F32)
    prob_grad = jnp.einsum("tjd,nd->jtn", attended_grad, value_rows, preferred_element_type=F32)
    row_dot = jnp.sum(attended_grad.astype(F32) * attended.astype(F32), axis=-1).T
    score_grad = (probs_full * (prob_grad - row_dot[..., None]) * scale_factor).astype(BF)
    query_grad = jnp.einsum("jtn,nd->tjd", score_grad, key_rows, preferred_element_type=F32)
    key_grad = jnp.einsum("jtn,tjd->nd", score_grad, queries, preferred_element_type=F32)
    return query_grad, key_grad, value_grad


class Peers:
    def __init__(self, axis, size):
        self.axis = axis
        self.size = size
        self.paired = size & (size - 1) == 0
        self.me = lax.axis_index(axis)

    def to(self, index, step):
        return index ^ step if self.paired else (index + step) % self.size

    def source(self, step):
        return self.me ^ step if self.paired else (self.me - step + self.size) % self.size

    def spread(self, own):
        blocks = [own]
        for step in range(1, self.size):
            pairs = [(i, self.to(i, step)) for i in range(self.size)]
            blocks.append(lax.ppermute(own, self.axis, pairs))
        return blocks

    def exchange(self, parts):
        result = parts
        for step in range(1, self.size):
            source = self.source(step)
            pairs = [(self.to(i, step), i) for i in range(self.size)]
            got = lax.ppermute(lax.dynamic_index_in_dim(parts, source, 0), self.axis, pairs)
            target = source if self.paired else (self.me + step) % self.size
            result = lax.dynamic_update_slice_in_dim(result, got, target, 0)
        return result

    def shares(self, partial):
        return [partial(step).astype(BF) for step in range(self.size - 1, 0, -1)] + [partial(0)]

    def send(self, shares):
        received = shares[-1:]
        for step, share in zip(range(self.size - 1, 0, -1), shares):
            pairs = [(self.to(i, step), i) for i in range(self.size)]
            received.append(lax.ppermute(share, self.axis, pairs))
        return received

    def deliver(self, partial):
        return self.send(self.shares(partial))


def add_up(shares):
    return sum(share.astype(F32) for share in shares[1:]) + shares[0].astype(F32)


class Halves:
    def __init__(self, size):
        self.size = size

    def swap(self, own):
        return lax.ppermute(own, "far", [(i, self.size - 1 - i) for i in range(self.size)])


def pad_to(values, axis, size):
    widths = [(0, 0)] * values.ndim
    widths[axis] = (0, size - values.shape[axis])
    return jnp.pad(values, widths)


def round_up(value, unit):
    return -(-value // unit) * unit


class HeadSplit:
    def __init__(self, peers, dp_n, rows, bias_rows):
        self.peers = peers
        self.n = peers.size
        self.dp_n = dp_n
        self.rows = rows
        self.bias_rows = bias_rows
        self.share = self.n // KV
        self.heads = H // self.n
        self.q_cols = self.heads * HD
        self.cols = self.q_cols + 2 * HD
        self.bias_cols = -(-bias_rows // rows)
        self.width = self.cols + round_up(2 + self.bias_cols, LANES)

    @staticmethod
    def fits(n):
        return n % KV == 0 and H % n == 0

    def slices(self, values):
        rows = values.shape[0]
        query = values[:, : H * HD].reshape(rows, self.n, self.q_cols)
        both = values[:, H * HD :].reshape(rows, 2, KV, 1, HD)
        both = jnp.broadcast_to(both, (rows, 2, KV, self.share, HD)).reshape(rows, 2, self.n, HD)
        return jnp.concatenate([query, both[:, 0], both[:, 1]], axis=2)

    def gather(self, attn_gain, mlp_gain, qkv_weight, qkv_bias, out_weight):
        rows, n, dp_n = self.rows, self.n, self.dp_n
        bias = pad_to(qkv_bias, 0, self.bias_cols * rows).reshape(self.bias_cols, rows)
        extra = jnp.concatenate([attn_gain[None], mlp_gain[None], bias], axis=0).T
        extra = pad_to(extra, 1, self.width - self.cols)
        extra = jnp.broadcast_to(extra[:, None], (rows, n, extra.shape[1]))
        pack = jnp.concatenate([self.slices(qkv_weight), extra], axis=2).transpose(1, 0, 2)
        pack = lax.all_to_all(pack, "ctx", 0, 0, tiled=True).reshape(n * rows, self.width)
        moves = [(b, (b % dp_n) * n + b // dp_n) for b in range(dp_n * n)]
        out_block = lax.ppermute(out_weight, ALL, moves)
        self.out_rows, self.out_cols = out_weight.shape
        self.extra_rows = self.out_rows * self.out_cols // self.width
        pack = jnp.concatenate([pack, out_block.reshape(self.extra_rows, self.width)], axis=0)
        whole = lax.all_gather(pack, DP, axis=0, tiled=False)
        joint = whole[:, : n * rows].reshape(dp_n * n * rows, self.width)
        self.out_slice = whole[:, n * rows :].reshape(dp_n * self.out_rows, self.out_cols)
        self.qkv_slice = joint[:, : self.cols]
        bias = joint[:, self.cols + 2 : self.cols + 2 + self.bias_cols]
        bias = bias.reshape(dp_n * n, rows, self.bias_cols).transpose(0, 2, 1)
        bias = bias.reshape(dp_n * n, self.bias_cols * rows)[:, : self.bias_rows].reshape(-1)
        self.bias_slice = jnp.concatenate(
            [lax.dynamic_slice(bias, (start,), (size,)) for start, size in self.places()]
        ).astype(F32)
        return joint[:, self.cols].astype(F32), joint[:, self.cols + 1].astype(F32)

    def places(self):
        me = self.peers.me
        group = me // self.share
        return (
            (me * self.q_cols, self.q_cols),
            (H * HD + group * HD, HD),
            (H * HD + KV * HD + group * HD, HD),
        )

    def forward(self, blocks, segment_ids, gain, before):
        peers, n = self.peers, self.n
        span = blocks[0].shape[0]
        length = n * span
        starts = [peers.source(step) * span for step in range(n)]
        index = jnp.concatenate([start + jnp.arange(span, dtype=jnp.int32) for start in starts])
        segments = jnp.concatenate(peers.spread(segment_ids), axis=1)[0]
        doc_start = jnp.sum((segments[None, :] < segments[:, None]).astype(jnp.int32), axis=1)
        self.cos_table, self.sin_table = rope_tables(index - doc_start)
        self.visible = (index[None, :] <= index[:, None]) & (
            segments[None, :] == segments[:, None]
        )
        self.scale = 1.0 / math.sqrt(HD)
        self.resid = jnp.concatenate(blocks).astype(F32)
        self.inv = inv_rms_of(self.resid)
        self.normed = (self.resid * self.inv * gain).astype(BF)
        projected = dot(self.normed, self.qkv_slice) + self.bias_slice
        query_pre = projected[:, : self.q_cols].reshape(length, self.heads, HD)
        key_pre = projected[:, self.q_cols : self.q_cols + HD].reshape(length, 1, HD)
        self.values = projected[:, self.q_cols + HD :].astype(BF)
        self.query = rotate(query_pre, self.cos_table, self.sin_table).astype(BF)
        self.key = rotate(key_pre, self.cos_table, self.sin_table).astype(BF).reshape(length, HD)
        attended, self.log_total = attend(
            self.query, self.key, self.values, self.visible, self.scale
        )
        self.attended, before = lax.optimization_barrier((attended.astype(BF), before))
        flat = self.attended.reshape(length, self.q_cols)
        mixed = add_up(
            peers.deliver(lambda step: dot(flat[step * span : (step + 1) * span], self.out_slice))
        )
        return blocks[0].astype(F32) + mixed, before

    def backward(self, mid_grad, gain, gain_two_term, filler, after):
        peers, n, rows, dp_n = self.peers, self.n, self.rows, self.dp_n
        span = mid_grad.shape[0]
        blocks, filled = lax.optimization_barrier((peers.spread(mid_grad.astype(BF)), filler()))
        after = (after, filled)
        low = jnp.concatenate(blocks)
        length = low.shape[0]
        attended_grad = dot_t(low, self.out_slice).astype(BF).reshape(length, self.heads, HD)
        out_term = t_dot(self.attended.reshape(length, self.q_cols), low)
        query_grad, key_grad, value_grad = attend_back(
            self.query,
            self.key,
            self.values,
            self.visible,
            self.attended,
            attended_grad,
            self.log_total,
            self.scale,
        )
        query_grad = rotate(query_grad, self.cos_table, -self.sin_table).reshape(length, -1)
        key_grad = rotate(key_grad[:, None], self.cos_table, -self.sin_table).reshape(length, HD)
        proj_grad = jnp.concatenate([query_grad, key_grad, value_grad], axis=1)
        bias_term = jnp.sum(proj_grad, axis=0)
        low_grad = proj_grad.astype(BF)
        qkv_term = t_dot(self.normed, low_grad)
        gain_terms = []

        def share(step):
            part = slice(step * span, (step + 1) * span)
            normed_grad = dot_t(low_grad[part], self.qkv_slice)
            gain_terms.append(jnp.sum(normed_grad * (self.resid[part] * self.inv[part]), axis=0))
            return normed_grad

        normed_shares = peers.deliver(share)
        qkv_term, out_term = qkv_term.astype(BF), out_term.astype(BF)
        normed_grad = add_up(normed_shares)
        own = slice(0, span)
        input_grad = mid_grad + norm_back(normed_grad, self.resid[own], self.inv[own], gain)
        bias = jnp.zeros((dp_n * n * self.bias_rows,), F32)
        first = 0
        for start, size in self.places():
            bias = lax.dynamic_update_slice(bias, bias_term[first : first + size], (start,))
            first += size
        bias = pad_to(bias.reshape(dp_n * n, self.bias_rows), 1, self.bias_cols * rows)
        bias = bias.reshape(dp_n * n, self.bias_cols, rows).transpose(1, 0, 2)
        extra = jnp.concatenate(
            [sum(gain_terms)[None], gain_two_term[None], bias.reshape(self.bias_cols, -1)], axis=0
        ).T
        extra = pad_to(extra, 1, self.width - self.cols)
        joint = jnp.concatenate([qkv_term, extra.astype(BF)], axis=1)
        joint = joint.reshape(dp_n, n * rows, self.width)
        out_term = out_term.reshape(dp_n, self.extra_rows, self.width)
        pack, filled = lax.optimization_barrier((jnp.concatenate([joint, out_term], axis=1), after))
        mine = lax.psum_scatter(pack, DP, scatter_dimension=0, tiled=False)
        moves = [((b % dp_n) * n + b // dp_n, b) for b in range(dp_n * n)]
        out_grad = lax.ppermute(
            mine[n * rows :].reshape(self.out_rows, self.out_cols), ALL, moves
        ).astype(F32)
        parts = lax.all_to_all(
            mine[: n * rows].reshape(n, rows, self.width), "ctx", 0, 0, tiled=True
        ).astype(F32)
        query = parts[:, :, : self.q_cols].transpose(1, 0, 2).reshape(rows, -1)
        both = parts[:, :, self.q_cols : self.cols].reshape(KV, self.share, rows, 2, HD)
        both = jnp.sum(both, axis=1).transpose(1, 2, 0, 3).reshape(rows, -1)
        extra = jnp.sum(parts[:, :, self.cols :], axis=0)
        bias_grad = extra[:, 2 : 2 + self.bias_cols].T.reshape(-1)[: self.bias_rows]
        return (
            input_grad,
            extra[:, 0],
            jnp.concatenate([query, both], axis=1),
            bias_grad,
            out_grad,
            extra[:, 1],
        ), filled


class RowSplit:
    def __init__(self, peers):
        self.peers = peers

    def gather(self, attn_gain, mlp_gain, qkv_weight, qkv_bias, out_weight):
        gain_one, gain_two, self.qkv, bias, self.out = (
            lax.all_gather(part, ALL, axis=0, tiled=True)
            for part in (attn_gain, mlp_gain, qkv_weight, qkv_bias, out_weight)
        )
        self.bias = bias.astype(F32)
        return gain_one.astype(F32), gain_two.astype(F32)

    def forward(self, blocks, segment_ids, gain, before):
        own = blocks[0]
        span = own.shape[0]
        width = KV * HD
        segments = segment_ids[0]
        all_segments = lax.all_gather(segment_ids, "ctx", axis=1, tiled=True)[0]
        length = all_segments.shape[0]
        query_index = self.peers.me * span + jnp.arange(span, dtype=jnp.int32)
        key_index = jnp.arange(length, dtype=jnp.int32)
        doc_start = jnp.sum((all_segments[None] < segments[:, None]).astype(jnp.int32), axis=1)
        self.cos_table, self.sin_table = rope_tables(query_index - doc_start)
        self.visible = (key_index[None, :] <= query_index[:, None]) & (
            all_segments[None, :] == segments[:, None]
        )
        self.scale = 1.0 / math.sqrt(HD)
        self.resid = own.astype(F32)
        self.inv = inv_rms_of(self.resid)
        self.normed = (self.resid * self.inv * gain).astype(BF)
        projected = dot(self.normed, self.qkv) + self.bias
        query_pre = projected[:, : H * HD].reshape(span, H, HD)
        key_pre = projected[:, H * HD : H * HD + width].reshape(span, KV, HD)
        values = projected[:, H * HD + width :].astype(BF)
        self.query = rotate(query_pre, self.cos_table, self.sin_table).astype(BF)
        key_rot = rotate(key_pre, self.cos_table, self.sin_table).astype(BF).reshape(span, width)
        self.key, self.values = (
            lax.all_gather(part, "ctx", axis=0, tiled=True).reshape(length, KV, HD)
            for part in (key_rot, values)
        )
        pieces = [
            attend(
                self.query[:, self.part(group)],
                self.key[:, group],
                self.values[:, group],
                self.visible,
                self.scale,
            )
            for group in range(KV)
        ]
        self.attended = jnp.concatenate([piece[0] for piece in pieces], axis=1).astype(BF)
        self.log_totals = [piece[1] for piece in pieces]
        return self.resid + dot(self.attended.reshape(span, -1), self.out), before

    @staticmethod
    def part(group):
        return slice(group * (H // KV), (group + 1) * (H // KV))

    def backward(self, mid_grad, gain, gain_two_term, filler, after):
        span = mid_grad.shape[0]
        low = mid_grad.astype(BF)
        attended_grad = dot_t(low, self.out).astype(BF).reshape(span, H, HD)
        grads = [
            attend_back(
                self.query[:, self.part(group)],
                self.key[:, group],
                self.values[:, group],
                self.visible,
                self.attended[:, self.part(group)],
                attended_grad[:, self.part(group)],
                self.log_totals[group],
                self.scale,
            )
            for group in range(KV)
        ]
        query_grad = jnp.concatenate([grad[0] for grad in grads], axis=1)
        key_grad, value_grad = (
            lax.psum_scatter(
                jnp.concatenate([grad[place] for grad in grads], axis=1).astype(BF),
                "ctx",
                scatter_dimension=0,
                tiled=True,
            ).astype(F32)
            for place in (1, 2)
        )
        query_grad = rotate(query_grad, self.cos_table, -self.sin_table).reshape(span, -1)
        key_grad = rotate(key_grad.reshape(span, KV, HD), self.cos_table, -self.sin_table)
        proj_grad = jnp.concatenate([query_grad, key_grad.reshape(span, -1), value_grad], axis=1)
        low_grad = proj_grad.astype(BF)
        normed_grad = dot_t(low_grad, self.qkv)
        input_grad = mid_grad + norm_back(normed_grad, self.resid, self.inv, gain)
        gain_term = jnp.sum(normed_grad * (self.resid * self.inv), axis=0)
        terms = (
            gain_term,
            t_dot(self.normed, low_grad).astype(BF),
            jnp.sum(proj_grad, axis=0),
            t_dot(self.attended.reshape(span, -1), low).astype(BF),
            gain_two_term,
        )
        grads = (input_grad,) + tuple(
            lax.psum_scatter(term, ALL, scatter_dimension=0, tiled=True).astype(F32)
            for term in terms
        )
        return grads, (after, filler())


def on_device(
    inputs,
    cotangent,
    segment_ids,
    attn_gain,
    qkv_weight,
    qkv_bias,
    out_weight,
    mlp_gain,
    gate_weight,
    up_weight,
    down_weight,
    *,
    far_n,
    near_n,
    ctx_n,
):
    span, features = inputs.shape[1:]
    rows, hidden_width = gate_weight.shape
    n = ctx_n
    dp_n = far_n * near_n
    peers = Peers("ctx", n)
    halves = Halves(far_n)
    if HeadSplit.fits(n):
        attention = HeadSplit(peers, dp_n, rows, qkv_bias.shape[0])
        blocks = peers.spread(inputs[0])
    else:
        attention = RowSplit(peers)
        blocks = [inputs[0]]
    gain_one, gain_two = attention.gather(attn_gain, mlp_gain, qkv_weight, qkv_bias, out_weight)

    unit = hidden_width // (dp_n * n)
    width = near_n * unit
    wide = round_up(width, LANES)
    places = far_n * n

    def column_slices(weight):
        parts = weight.reshape(rows, far_n, near_n, n, unit).transpose(1, 3, 0, 2, 4)
        return pad_to(parts.reshape(places, rows, width), 2, wide)

    def weight_columns(values):
        parts = values.reshape(far_n, n, rows, near_n, unit).transpose(2, 0, 3, 1, 4)
        return parts.reshape(rows, hidden_width).astype(F32)

    joint = jnp.concatenate([column_slices(gate_weight), column_slices(up_weight)], axis=2)
    if far_n == 1:
        joint = peers.exchange(joint)
    else:
        joint = lax.all_to_all(joint, ("far", "ctx"), 0, 0, tiled=True)
    gate_up = lax.all_gather(joint.reshape(places * rows, 2 * wide), "near", axis=0, tiled=True)
    down = lax.all_gather(down_weight, "near", axis=0, tiled=True)

    def to_gathered(values):
        parts = values.reshape(span, far_n, near_n, -1).transpose(0, 2, 1, 3)
        return parts.reshape(span, features)

    def from_gathered(values):
        parts = values.reshape(span, near_n, far_n, -1).transpose(0, 2, 1, 3)
        return parts.reshape(span, features)

    def spread_wide(own):
        return sum([peers.spread(own if far == 0 else halves.swap(own)) for far in range(far_n)], [])

    def block(values, far, step):
        start = (far * n + step) * span
        return values[start : start + span]

    grad_out = spread_wide(cotangent[0])
    resid_mid, grad_out = attention.forward(blocks, segment_ids, gain_one, grad_out)
    inv_two = inv_rms_of(resid_mid)
    normed_own = (resid_mid * inv_two * gain_two).astype(BF)
    normed = jnp.concatenate(spread_wide(to_gathered(normed_own)))
    grad_out = jnp.concatenate(grad_out)
    pre = dot(normed, gate_up)
    gate_pre = pre[:, :width]
    up_pre = pre[:, wide : wide + width]
    sigmoid_gate = jax.nn.sigmoid(gate_pre)
    silu_gate = gate_pre * sigmoid_gate
    hidden = (silu_gate * up_pre).astype(BF)
    down_term = t_dot(hidden, grad_out).astype(BF)
    down_term, grad_out = lax.optimization_barrier((down_term, grad_out))
    down_grad = lax.psum_scatter(down_term, "near", scatter_dimension=0, tiled=True)
    hidden_grad = dot_t(grad_out, down)
    gate_grad = (
        hidden_grad * up_pre * sigmoid_gate * (1.0 + gate_pre * (1.0 - sigmoid_gate))
    ).astype(BF)
    up_grad = (hidden_grad * silu_gate).astype(BF)
    pre_grad = jnp.concatenate([pad_to(gate_grad, 1, wide), pad_to(up_grad, 1, wide)], axis=1)
    shares = [
        peers.deliver(lambda step: dot_t(block(pre_grad, far, step), gate_up))
        for far in range(far_n - 1, -1, -1)
    ]
    joint_term = t_dot(normed, pre_grad).astype(BF)
    shares, joint_term = lax.optimization_barrier((shares, joint_term))
    joint_term, down_grad = lax.optimization_barrier((joint_term, down_grad))
    joint_grad = lax.psum_scatter(joint_term, "near", scatter_dimension=0, tiled=True)
    def combine(shares):
        if far_n == 1:
            return add_up(shares[0])
        swapped = halves.swap(add_up(shares[0]).astype(BF))
        return add_up(shares[1] + [swapped])

    def output_shares():
        return [
            peers.shares(lambda step: dot(block(hidden, far, step), down))
            for far in range(far_n - 1, -1, -1)
        ]

    normed_two_grad = from_gathered(combine(shares))
    normed_two = resid_mid * inv_two
    gain_two_term = jnp.sum(normed_two_grad * normed_two, axis=0)
    mid_grad = cotangent[0].astype(F32) + norm_back(normed_two_grad, resid_mid, inv_two, gain_two)
    grads, (joint_grad, out_shares) = attention.backward(
        mid_grad, gain_one, gain_two_term, output_shares, joint_grad
    )
    joint_grad = lax.all_to_all(
        joint_grad.reshape(places, rows, 2 * wide), ("far", "ctx"), 0, 0, tiled=True
    )
    gate_weight_grad = weight_columns(joint_grad[:, :, :width])
    up_weight_grad = weight_columns(joint_grad[:, :, wide : wide + width])
    input_grad, attn_gain_grad, qkv_weight_grad, qkv_bias_grad, out_weight_grad, mlp_gain_grad = (
        grads
    )
    output = resid_mid + combine([peers.send(shares) for shares in out_shares])
    return (
        output.astype(BF)[None],
        input_grad[None],
        attn_gain_grad,
        qkv_weight_grad,
        qkv_bias_grad,
        out_weight_grad,
        mlp_gain_grad,
        gate_weight_grad,
        up_weight_grad,
        down_grad.astype(F32),
    )


def solution(mesh):
    dp_n, ctx_n = mesh.shape["dp"], mesh.shape["ctx"]
    far_n = 1
    split = jax.sharding.Mesh(mesh.devices.reshape(far_n, dp_n // far_n, ctx_n), ALL)
    body = functools.partial(on_device, far_n=far_n, near_n=dp_n // far_n, ctx_n=ctx_n)
    return jax.shard_map(
        body,
        mesh=split,
        in_specs=(
            P(DP, "ctx", None),
            P(DP, "ctx", None),
            P(DP, "ctx"),
            P(ALL),
            P(ALL, None),
            P(ALL),
            P(ALL, None),
            P(ALL),
            P(ALL, None),
            P(ALL, None),
            P(ALL, None),
        ),
        out_specs=(
            P(DP, "ctx", None),
            P(DP, "ctx", None),
            P(ALL),
            P(ALL, None),
            P(ALL),
            P(ALL, None),
            P(ALL),
            P(ALL, None),
            P(ALL, None),
            P(ALL, None),
        ),
        check_vma=False,
    )
```

```python
import functools
import math

import jax
import jax.numpy as jnp
from jax import lax
from jax.sharding import PartitionSpec as P

H = 12
KV = 2
HD = 128
LANES = 128


EPS = 1e-06
THETA = 1000000.0
MASKED = -1e30
BF = jnp.bfloat16
F32 = jnp.float32
ALL = ("dp", "ctx")


def rope_tables(positions):
    half_dim = jnp.arange(0, HD, 2).astype(F32) / HD
    inverse = THETA ** (-half_dim)
    angles = positions.astype(F32)[:, None] * inverse[None, :]
    angles = jnp.concatenate([angles, angles], axis=1)
    return (jnp.cos(angles), jnp.sin(angles))


def rotate(values, cos_table, sin_table):
    half_dim = values.shape[-1] // 2
    turned = jnp.concatenate([-values[..., half_dim:], values[..., :half_dim]], axis=-1)
    return values * cos_table[:, None, :] + turned * sin_table[:, None, :]


def inv_rms_of(values):
    return lax.rsqrt(jnp.mean(values * values, axis=-1, keepdims=True) + EPS)


def norm_back(normed_grad, values, inv_rms, gain):
    normed = values * inv_rms
    scaled_grad = normed_grad * gain
    return inv_rms * (scaled_grad - normed * jnp.mean(scaled_grad * normed, axis=-1, keepdims=True))


def dot(a, b):
    return jnp.dot(a, b, preferred_element_type=F32)


def dot_t(a, b):
    return lax.dot_general(a, b, (((1,), (1,)), ((), ())), preferred_element_type=F32)


def t_dot(a, b):
    return lax.dot_general(a, b, (((0,), (0,)), ((), ())), preferred_element_type=F32)


def attend(queries, key_rows, value_rows, visible, scale_factor):
    scores = jnp.einsum("tjd,nd->jtn", queries, key_rows, preferred_element_type=F32) * scale_factor
    scores = jnp.where(visible[None], scores, MASKED)
    row_max = jnp.max(scores, axis=-1, keepdims=True)
    row_sum = jnp.sum(jnp.exp(scores - row_max), axis=-1, keepdims=True)
    log_total = row_max + jnp.log(row_sum)
    weights = jnp.exp(scores - log_total).astype(BF)
    mixed = jnp.einsum("jtn,nd->tjd", weights, value_rows, preferred_element_type=F32)
    return mixed, log_total


def attend_back(
    queries, key_rows, value_rows, visible, attended, attended_grad, log_total, scale_factor
):
    scores = jnp.einsum("tjd,nd->jtn", queries, key_rows, preferred_element_type=F32) * scale_factor
    scores = jnp.where(visible[None], scores, MASKED)
    probs_full = jnp.exp(scores - log_total)
    probs_low = probs_full.astype(BF)
    value_grad = jnp.einsum("jtn,tjd->nd", probs_low, attended_grad, preferred_element_type=F32)
    prob_grad = jnp.einsum("tjd,nd->jtn", attended_grad, value_rows, preferred_element_type=F32)
    row_dot = jnp.sum(attended_grad.astype(F32) * attended.astype(F32), axis=-1).T
    score_grad = (probs_full * (prob_grad - row_dot[..., None]) * scale_factor).astype(BF)
    query_grad = jnp.einsum("jtn,nd->tjd", score_grad, key_rows, preferred_element_type=F32)
    key_grad = jnp.einsum("jtn,tjd->nd", score_grad, queries, preferred_element_type=F32)
    return query_grad, key_grad, value_grad


class Peers:
    def __init__(self, axis, size):
        self.axis = axis
        self.size = size
        self.paired = size & (size - 1) == 0
        self.me = lax.axis_index(axis)

    def to(self, index, step):
        return index ^ step if self.paired else (index + step) % self.size

    def source(self, step):
        return self.me ^ step if self.paired else (self.me - step + self.size) % self.size

    def spread(self, own):
        blocks = [own]
        for step in range(1, self.size):
            pairs = [(i, self.to(i, step)) for i in range(self.size)]
            blocks.append(lax.ppermute(own, self.axis, pairs))
        return blocks

    def exchange(self, parts):
        result = parts
        for step in range(1, self.size):
            source = self.source(step)
            pairs = [(self.to(i, step), i) for i in range(self.size)]
            got = lax.ppermute(lax.dynamic_index_in_dim(parts, source, 0), self.axis, pairs)
            target = source if self.paired else (self.me + step) % self.size
            result = lax.dynamic_update_slice_in_dim(result, got, target, 0)
        return result

    def deliver(self, partial):
        span = partial.shape[0] // self.size
        received = [partial[:span]]
        for step in range(self.size - 1, 0, -1):
            pairs = [(self.to(i, step), i) for i in range(self.size)]
            share = partial[step * span : (step + 1) * span]
            received.append(lax.ppermute(share, self.axis, pairs))
        return received


def add_up(shares):
    return sum(share.astype(F32) for share in shares[1:]) + shares[0].astype(F32)


def pad_to(values, axis, size):
    widths = [(0, 0)] * values.ndim
    widths[axis] = (0, size - values.shape[axis])
    return jnp.pad(values, widths)


def round_up(value, unit):
    return -(-value // unit) * unit


class HeadSplit:
    def __init__(self, peers, dp_n, rows, bias_rows):
        self.peers = peers
        self.n = peers.size
        self.dp_n = dp_n
        self.rows = rows
        self.bias_rows = bias_rows
        self.share = self.n // KV
        self.heads = H // self.n
        self.q_cols = self.heads * HD
        self.cols = self.q_cols + 2 * HD
        self.bias_cols = -(-bias_rows // rows)
        self.width = self.cols + round_up(2 + self.bias_cols, LANES)

    @staticmethod
    def fits(n):
        return n % KV == 0 and H % n == 0

    def slices(self, values):
        rows = values.shape[0]
        query = values[:, : H * HD].reshape(rows, self.n, self.q_cols)
        both = values[:, H * HD :].reshape(rows, 2, KV, 1, HD)
        both = jnp.broadcast_to(both, (rows, 2, KV, self.share, HD)).reshape(rows, 2, self.n, HD)
        return jnp.concatenate([query, both[:, 0], both[:, 1]], axis=2)

    def gather(self, attn_gain, mlp_gain, qkv_weight, qkv_bias, out_weight):
        rows, n, dp_n = self.rows, self.n, self.dp_n
        bias = pad_to(qkv_bias, 0, self.bias_cols * rows).reshape(self.bias_cols, rows)
        extra = jnp.concatenate([attn_gain[None], mlp_gain[None], bias], axis=0).T
        extra = pad_to(extra, 1, self.width - self.cols)
        extra = jnp.broadcast_to(extra[:, None], (rows, n, extra.shape[1]))
        pack = jnp.concatenate([self.slices(qkv_weight), extra], axis=2).transpose(1, 0, 2)
        pack = lax.all_to_all(pack, "ctx", 0, 0, tiled=True).reshape(n * rows, self.width)
        moves = [(b, (b % dp_n) * n + b // dp_n) for b in range(dp_n * n)]
        out_block = lax.ppermute(out_weight, ALL, moves)
        self.out_rows, self.out_cols = out_weight.shape
        self.extra_rows = self.out_rows * self.out_cols // self.width
        pack = jnp.concatenate([pack, out_block.reshape(self.extra_rows, self.width)], axis=0)
        whole = lax.all_gather(pack, "dp", axis=0, tiled=False)
        joint = whole[:, : n * rows].reshape(dp_n * n * rows, self.width)
        self.out_slice = whole[:, n * rows :].reshape(dp_n * self.out_rows, self.out_cols)
        self.joint = joint
        bias = joint[:, self.cols + 2 : self.cols + 2 + self.bias_cols]
        bias = bias.reshape(dp_n * n, rows, self.bias_cols).transpose(0, 2, 1)
        bias = bias.reshape(dp_n * n, self.bias_cols * rows)[:, : self.bias_rows].reshape(-1)
        self.bias_slice = jnp.concatenate(
            [lax.dynamic_slice(bias, (start,), (size,)) for start, size in self.places()]
        ).astype(F32)
        return joint[:, self.cols].astype(F32), joint[:, self.cols + 1].astype(F32)

    def places(self):
        me = self.peers.me
        group = me // self.share
        return (
            (me * self.q_cols, self.q_cols),
            (H * HD + group * HD, HD),
            (H * HD + KV * HD + group * HD, HD),
        )

    def forward(self, blocks, segment_ids, gain, before):
        peers, n = self.peers, self.n
        span = blocks[0].shape[0]
        length = n * span
        starts = [peers.source(step) * span for step in range(n)]
        index = jnp.concatenate([start + jnp.arange(span, dtype=jnp.int32) for start in starts])
        segments = jnp.concatenate(peers.spread(segment_ids), axis=1)[0]
        doc_start = jnp.sum((segments[None, :] < segments[:, None]).astype(jnp.int32), axis=1)
        self.cos_table, self.sin_table = rope_tables(index - doc_start)
        self.visible = (index[None, :] <= index[:, None]) & (
            segments[None, :] == segments[:, None]
        )
        self.scale = 1.0 / math.sqrt(HD)
        self.resid = jnp.concatenate(blocks).astype(F32)
        self.inv = inv_rms_of(self.resid)
        self.normed = (self.resid * self.inv * gain).astype(BF)
        projected = dot(self.normed, self.joint)[:, : self.cols] + self.bias_slice
        query_pre = projected[:, : self.q_cols].reshape(length, self.heads, HD)
        key_pre = projected[:, self.q_cols : self.q_cols + HD].reshape(length, 1, HD)
        self.values = projected[:, self.q_cols + HD : self.cols].astype(BF)
        self.query = rotate(query_pre, self.cos_table, self.sin_table).astype(BF)
        self.key = rotate(key_pre, self.cos_table, self.sin_table).astype(BF).reshape(length, HD)
        attended, self.log_total = attend(
            self.query, self.key, self.values, self.visible, self.scale
        )
        self.attended, before = lax.optimization_barrier((attended.astype(BF), before))
        flat = self.attended.reshape(length, self.q_cols)
        mixed = add_up(peers.deliver(dot(flat, self.out_slice).astype(BF)))
        return blocks[0].astype(F32) + mixed, before

    def backward(self, mid_grad, gain, gain_two_term, filled, joint_grad, finish):
        peers, n, rows, dp_n = self.peers, self.n, self.rows, self.dp_n
        span = mid_grad.shape[0]
        blocks, filled = lax.optimization_barrier((peers.spread(mid_grad.astype(BF)), filled))
        filled = peers.deliver(filled)
        low = jnp.concatenate(blocks)
        length = low.shape[0]
        attended_grad = dot_t(low, self.out_slice).astype(BF).reshape(length, self.heads, HD)
        out_term = t_dot(self.attended.reshape(length, self.q_cols), low)
        query_grad, key_grad, value_grad = attend_back(
            self.query,
            self.key,
            self.values,
            self.visible,
            self.attended,
            attended_grad,
            self.log_total,
            self.scale,
        )
        query_grad = rotate(query_grad, self.cos_table, -self.sin_table).reshape(length, -1)
        key_grad = rotate(key_grad[:, None], self.cos_table, -self.sin_table).reshape(length, HD)
        proj_grad = jnp.concatenate([query_grad, key_grad, value_grad], axis=1)
        bias_term = jnp.sum(proj_grad, axis=0)
        low_grad = pad_to(proj_grad.astype(BF), 1, self.width)
        partial = dot_t(low_grad, self.joint).astype(BF)
        partial, filled = lax.optimization_barrier((partial, filled))
        normed_shares = peers.deliver(partial)
        gain_term = jnp.sum(partial.astype(F32) * (self.resid * self.inv), axis=0)
        qkv_term = t_dot(self.normed, low_grad)
        bias = jnp.zeros((dp_n * n * self.bias_rows,), F32)
        first = 0
        for start, size in self.places():
            bias = lax.dynamic_update_slice(bias, bias_term[first : first + size], (start,))
            first += size
        bias = pad_to(bias.reshape(dp_n * n, self.bias_rows), 1, self.bias_cols * rows)
        bias = bias.reshape(dp_n * n, self.bias_cols, rows).transpose(1, 0, 2)
        extra = jnp.concatenate(
            [gain_term[None], gain_two_term[None], bias.reshape(self.bias_cols, -1)], axis=0
        ).T
        extra = jnp.pad(extra, ((0, 0), (self.cols, self.width - self.cols - extra.shape[1])))
        joint = (qkv_term + extra).astype(BF).reshape(dp_n, n * rows, self.width)
        out_term = out_term.astype(BF).reshape(dp_n, self.extra_rows, self.width)
        pack, joint_grad, normed_shares = lax.optimization_barrier(
            (jnp.concatenate([joint, out_term], axis=1), joint_grad, normed_shares)
        )
        mine = lax.psum_scatter(pack, "dp", scatter_dimension=0, tiled=False)
        own = slice(0, span)
        normed_grad = add_up(normed_shares)
        input_grad = mid_grad + norm_back(normed_grad, self.resid[own], self.inv[own], gain)
        mine, output, finished = lax.optimization_barrier((mine, *finish(filled, joint_grad)))
        moves = [((b % dp_n) * n + b // dp_n, b) for b in range(dp_n * n)]
        out_grad = lax.ppermute(
            mine[n * rows :].reshape(self.out_rows, self.out_cols), ALL, moves
        ).astype(F32)
        parts = lax.all_to_all(
            mine[: n * rows].reshape(n, rows, self.width), "ctx", 0, 0, tiled=True
        ).astype(F32)
        query = parts[:, :, : self.q_cols].transpose(1, 0, 2).reshape(rows, -1)
        both = parts[:, :, self.q_cols : self.cols].reshape(KV, self.share, rows, 2, HD)
        both = jnp.sum(both, axis=1).transpose(1, 2, 0, 3).reshape(rows, -1)
        extra = jnp.sum(parts[:, :, self.cols :], axis=0)
        bias_grad = extra[:, 2 : 2 + self.bias_cols].T.reshape(-1)[: self.bias_rows]
        return (
            input_grad,
            extra[:, 0],
            jnp.concatenate([query, both], axis=1),
            bias_grad,
            out_grad,
            extra[:, 1],
        ), output, finished


class RowSplit:
    def __init__(self, peers):
        self.peers = peers

    def gather(self, attn_gain, mlp_gain, qkv_weight, qkv_bias, out_weight):
        gain_one, gain_two, self.qkv, bias, self.out = (
            lax.all_gather(part, ALL, axis=0, tiled=True)
            for part in (attn_gain, mlp_gain, qkv_weight, qkv_bias, out_weight)
        )
        self.bias = bias.astype(F32)
        return gain_one.astype(F32), gain_two.astype(F32)

    def forward(self, blocks, segment_ids, gain, before):
        own = blocks[0]
        span = own.shape[0]
        width = KV * HD
        segments = segment_ids[0]
        all_segments = lax.all_gather(segment_ids, "ctx", axis=1, tiled=True)[0]
        length = all_segments.shape[0]
        query_index = self.peers.me * span + jnp.arange(span, dtype=jnp.int32)
        key_index = jnp.arange(length, dtype=jnp.int32)
        doc_start = jnp.sum((all_segments[None] < segments[:, None]).astype(jnp.int32), axis=1)
        self.cos_table, self.sin_table = rope_tables(query_index - doc_start)
        self.visible = (key_index[None, :] <= query_index[:, None]) & (
            all_segments[None, :] == segments[:, None]
        )
        self.scale = 1.0 / math.sqrt(HD)
        self.resid = own.astype(F32)
        self.inv = inv_rms_of(self.resid)
        self.normed = (self.resid * self.inv * gain).astype(BF)
        projected = dot(self.normed, self.qkv) + self.bias
        query_pre = projected[:, : H * HD].reshape(span, H, HD)
        key_pre = projected[:, H * HD : H * HD + width].reshape(span, KV, HD)
        values = projected[:, H * HD + width :].astype(BF)
        self.query = rotate(query_pre, self.cos_table, self.sin_table).astype(BF)
        key_rot = rotate(key_pre, self.cos_table, self.sin_table).astype(BF).reshape(span, width)
        self.key, self.values = (
            lax.all_gather(part, "ctx", axis=0, tiled=True).reshape(length, KV, HD)
            for part in (key_rot, values)
        )
        pieces = [
            attend(
                self.query[:, self.part(group)],
                self.key[:, group],
                self.values[:, group],
                self.visible,
                self.scale,
            )
            for group in range(KV)
        ]
        self.attended = jnp.concatenate([piece[0] for piece in pieces], axis=1).astype(BF)
        self.log_totals = [piece[1] for piece in pieces]
        return self.resid + dot(self.attended.reshape(span, -1), self.out), before

    @staticmethod
    def part(group):
        return slice(group * (H // KV), (group + 1) * (H // KV))

    def backward(self, mid_grad, gain, gain_two_term, filled, joint_grad, finish):
        span = mid_grad.shape[0]
        low = mid_grad.astype(BF)
        attended_grad = dot_t(low, self.out).astype(BF).reshape(span, H, HD)
        grads = [
            attend_back(
                self.query[:, self.part(group)],
                self.key[:, group],
                self.values[:, group],
                self.visible,
                self.attended[:, self.part(group)],
                attended_grad[:, self.part(group)],
                self.log_totals[group],
                self.scale,
            )
            for group in range(KV)
        ]
        query_grad = jnp.concatenate([grad[0] for grad in grads], axis=1)
        key_grad, value_grad = (
            lax.psum_scatter(
                jnp.concatenate([grad[place] for grad in grads], axis=1).astype(BF),
                "ctx",
                scatter_dimension=0,
                tiled=True,
            ).astype(F32)
            for place in (1, 2)
        )
        query_grad = rotate(query_grad, self.cos_table, -self.sin_table).reshape(span, -1)
        key_grad = rotate(key_grad.reshape(span, KV, HD), self.cos_table, -self.sin_table)
        proj_grad = jnp.concatenate([query_grad, key_grad.reshape(span, -1), value_grad], axis=1)
        low_grad = proj_grad.astype(BF)
        normed_grad = dot_t(low_grad, self.qkv)
        input_grad = mid_grad + norm_back(normed_grad, self.resid, self.inv, gain)
        gain_term = jnp.sum(normed_grad * (self.resid * self.inv), axis=0)
        terms = (
            gain_term,
            t_dot(self.normed, low_grad).astype(BF),
            jnp.sum(proj_grad, axis=0),
            t_dot(self.attended.reshape(span, -1), low).astype(BF),
            gain_two_term,
        )
        grads = (input_grad,) + tuple(
            lax.psum_scatter(term, ALL, scatter_dimension=0, tiled=True).astype(F32)
            for term in terms
        )
        return grads, *finish(self.peers.deliver(filled), joint_grad)


def on_device(
    inputs,
    cotangent,
    segment_ids,
    attn_gain,
    qkv_weight,
    qkv_bias,
    out_weight,
    mlp_gain,
    gate_weight,
    up_weight,
    down_weight,
    *,
    dp_n,
    ctx_n,
):
    rows, hidden_width = gate_weight.shape
    n = ctx_n
    peers = Peers("ctx", n)
    if HeadSplit.fits(n):
        attention = HeadSplit(peers, dp_n, rows, qkv_bias.shape[0])
        blocks = peers.spread(inputs[0])
    else:
        attention = RowSplit(peers)
        blocks = [inputs[0]]
    gain_one, gain_two = attention.gather(attn_gain, mlp_gain, qkv_weight, qkv_bias, out_weight)

    unit = hidden_width // (dp_n * n)
    padded = round_up(unit, LANES // math.gcd(LANES, dp_n))
    wide = dp_n * padded

    def column_slices(weight):
        parts = pad_to(weight.reshape(rows, dp_n, n, unit), 3, padded)
        return parts.transpose(2, 0, 1, 3).reshape(n, rows, wide)

    def weight_columns(values):
        parts = values.reshape(n, rows, dp_n, padded)[..., :unit].transpose(1, 2, 0, 3)
        return parts.reshape(rows, hidden_width).astype(F32)

    joint = jnp.concatenate([column_slices(gate_weight), column_slices(up_weight)], axis=2)
    joint = peers.exchange(joint).reshape(n * rows, 2 * wide)
    gate_up = lax.all_gather(joint, "dp", axis=0, tiled=True)
    down = lax.all_gather(pad_to(down_weight, 0, padded), "dp", axis=0, tiled=True)

    blocks, own_cotangent = lax.optimization_barrier((blocks, cotangent[0]))
    grad_out = peers.spread(own_cotangent)
    resid_mid, grad_out = attention.forward(blocks, segment_ids, gain_one, grad_out)
    inv_two = inv_rms_of(resid_mid)
    normed_own = (resid_mid * inv_two * gain_two).astype(BF)
    normed = jnp.concatenate(peers.spread(normed_own))
    grad_out = jnp.concatenate(grad_out)
    pre = dot(normed, gate_up)
    gate_pre = pre[:, :wide]
    up_pre = pre[:, wide:]
    sigmoid_gate = jax.nn.sigmoid(gate_pre)
    silu_gate = gate_pre * sigmoid_gate
    hidden = (silu_gate * up_pre).astype(BF)
    down_term = t_dot(hidden, grad_out).astype(BF)
    down_term, grad_out = lax.optimization_barrier((down_term, grad_out))
    down_grad = lax.psum_scatter(down_term, "dp", scatter_dimension=0, tiled=True)
    hidden_grad = dot_t(grad_out, down)
    gate_grad = (
        hidden_grad * up_pre * sigmoid_gate * (1.0 + gate_pre * (1.0 - sigmoid_gate))
    ).astype(BF)
    up_grad = (hidden_grad * silu_gate).astype(BF)
    pre_grad = jnp.concatenate([gate_grad, up_grad], axis=1)
    shares = peers.deliver(dot_t(pre_grad, gate_up).astype(BF))
    joint_term = t_dot(normed, pre_grad).astype(BF)
    shares, joint_term = lax.optimization_barrier((shares, joint_term))
    joint_term, down_grad = lax.optimization_barrier((joint_term, down_grad))
    joint_grad = lax.psum_scatter(joint_term, "dp", scatter_dimension=0, tiled=True)

    normed_two_grad = add_up(shares)
    gain_two_term = jnp.sum(normed_two_grad * (resid_mid * inv_two), axis=0)
    mid_grad = cotangent[0].astype(F32) + norm_back(normed_two_grad, resid_mid, inv_two, gain_two)

    def finish(output_shares, joint_grad):
        output = resid_mid + add_up(output_shares)
        parts = peers.exchange(joint_grad.reshape(n, rows, 2 * wide))
        grads = (weight_columns(parts[:, :, :wide]), weight_columns(parts[:, :, wide:]))
        return output.astype(BF), grads

    grads, output, (gate_weight_grad, up_weight_grad) = attention.backward(
        mid_grad, gain_one, gain_two_term, dot(hidden, down).astype(BF), joint_grad, finish
    )
    input_grad, attn_gain_grad, qkv_weight_grad, qkv_bias_grad, out_weight_grad, mlp_gain_grad = (
        grads
    )
    return (
        output[None],
        input_grad[None],
        attn_gain_grad,
        qkv_weight_grad,
        qkv_bias_grad,
        out_weight_grad,
        mlp_gain_grad,
        gate_weight_grad,
        up_weight_grad,
        down_grad[:unit].astype(F32),
    )


def solution(mesh):
    body = functools.partial(on_device, dp_n=mesh.shape["dp"], ctx_n=mesh.shape["ctx"])
    return jax.shard_map(
        body,
        mesh=mesh,
        in_specs=(
            P("dp", "ctx", None),
            P("dp", "ctx", None),
            P("dp", "ctx"),
            P(ALL),
            P(ALL, None),
            P(ALL),
            P(ALL, None),
            P(ALL),
            P(ALL, None),
            P(ALL, None),
            P(ALL, None),
        ),
        out_specs=(
            P("dp", "ctx", None),
            P("dp", "ctx", None),
            P(ALL),
            P(ALL, None),
            P(ALL),
            P(ALL, None),
            P(ALL),
            P(ALL, None),
            P(ALL, None),
            P(ALL, None),
        ),
        check_vma=False,
    )
```

```python
import functools
import math

import jax
import jax.numpy as jnp
from jax import lax
from jax.sharding import PartitionSpec as P

H = 12
KV = 2
HD = 128
LANES = 128


EPS = 1e-06
THETA = 1000000.0
MASKED = -1e30
BF = jnp.bfloat16
F32 = jnp.float32
ALL = ("dp", "ctx")


def rope_tables(positions):
    half_dim = jnp.arange(0, HD, 2).astype(F32) / HD
    inverse = THETA ** (-half_dim)
    angles = positions.astype(F32)[:, None] * inverse[None, :]
    angles = jnp.concatenate([angles, angles], axis=1)
    return (jnp.cos(angles), jnp.sin(angles))


def rotate(values, cos_table, sin_table):
    half_dim = values.shape[-1] // 2
    turned = jnp.concatenate([-values[..., half_dim:], values[..., :half_dim]], axis=-1)
    return values * cos_table[:, None, :] + turned * sin_table[:, None, :]


def inv_rms_of(values):
    return lax.rsqrt(jnp.mean(values * values, axis=-1, keepdims=True) + EPS)


def norm_back(normed_grad, values, inv_rms, gain):
    normed = values * inv_rms
    scaled_grad = normed_grad * gain
    return inv_rms * (scaled_grad - normed * jnp.mean(scaled_grad * normed, axis=-1, keepdims=True))


def dot(a, b):
    return jnp.dot(a, b, preferred_element_type=F32)


def dot_t(a, b):
    return lax.dot_general(a, b, (((1,), (1,)), ((), ())), preferred_element_type=F32)


def t_dot(a, b):
    return lax.dot_general(a, b, (((0,), (0,)), ((), ())), preferred_element_type=F32)


def attend(queries, key_rows, value_rows, visible, scale_factor):
    scores = jnp.einsum("tjd,nd->jtn", queries, key_rows, preferred_element_type=F32) * scale_factor
    scores = jnp.where(visible[None], scores, MASKED)
    row_max = jnp.max(scores, axis=-1, keepdims=True)
    row_sum = jnp.sum(jnp.exp(scores - row_max), axis=-1, keepdims=True)
    log_total = row_max + jnp.log(row_sum)
    weights = jnp.exp(scores - log_total).astype(BF)
    mixed = jnp.einsum("jtn,nd->tjd", weights, value_rows, preferred_element_type=F32)
    return mixed, log_total


def attend_back(
    queries, key_rows, value_rows, visible, attended, attended_grad, log_total, scale_factor
):
    scores = jnp.einsum("tjd,nd->jtn", queries, key_rows, preferred_element_type=F32) * scale_factor
    scores = jnp.where(visible[None], scores, MASKED)
    probs_full = jnp.exp(scores - log_total)
    probs_low = probs_full.astype(BF)
    value_grad = jnp.einsum("jtn,tjd->nd", probs_low, attended_grad, preferred_element_type=F32)
    prob_grad = jnp.einsum("tjd,nd->jtn", attended_grad, value_rows, preferred_element_type=F32)
    row_dot = jnp.sum(attended_grad.astype(F32) * attended.astype(F32), axis=-1).T
    score_grad = (probs_full * (prob_grad - row_dot[..., None]) * scale_factor).astype(BF)
    query_grad = jnp.einsum("jtn,nd->tjd", score_grad, key_rows, preferred_element_type=F32)
    key_grad = jnp.einsum("jtn,tjd->nd", score_grad, queries, preferred_element_type=F32)
    return query_grad, key_grad, value_grad


class Peers:
    def __init__(self, axis, size):
        self.axis = axis
        self.size = size
        self.paired = size & (size - 1) == 0
        self.me = lax.axis_index(axis)

    def to(self, index, step):
        return index ^ step if self.paired else (index + step) % self.size

    def source(self, step):
        return self.me ^ step if self.paired else (self.me - step + self.size) % self.size

    def spread(self, own):
        blocks = [own]
        for step in range(1, self.size):
            pairs = [(i, self.to(i, step)) for i in range(self.size)]
            blocks.append(lax.ppermute(own, self.axis, pairs))
        return blocks

    def exchange(self, parts):
        received = []
        for step in range(1, self.size):
            pairs = [(self.to(i, step), i) for i in range(self.size)]
            block = lax.dynamic_index_in_dim(parts, self.source(step), 0)
            received.append(lax.ppermute(block, self.axis, pairs))
        parts, received = lax.optimization_barrier((parts, received))
        for step, block in enumerate(received, 1):
            target = self.source(step) if self.paired else (self.me + step) % self.size
            parts = lax.dynamic_update_slice_in_dim(parts, block, target, 0)
        return parts

    def deliver(self, partial):
        span = partial.shape[0] // self.size
        received = [partial[:span]]
        for step in range(self.size - 1, 0, -1):
            pairs = [(self.to(i, step), i) for i in range(self.size)]
            share = partial[step * span : (step + 1) * span]
            received.append(lax.ppermute(share, self.axis, pairs))
        return received


def add_up(shares):
    return sum(share.astype(F32) for share in shares[1:]) + shares[0].astype(F32)


def pad_to(values, axis, size):
    widths = [(0, 0)] * values.ndim
    widths[axis] = (0, size - values.shape[axis])
    return jnp.pad(values, widths)


def round_up(value, unit):
    return -(-value // unit) * unit


class HeadSplit:
    def __init__(self, peers, dp_n, rows, bias_rows):
        self.peers = peers
        self.n = peers.size
        self.dp_n = dp_n
        self.rows = rows
        self.bias_rows = bias_rows
        self.share = self.n // KV
        self.heads = H // self.n
        self.q_cols = self.heads * HD
        self.cols = self.q_cols + 2 * HD
        self.bias_cols = -(-bias_rows // rows)
        self.width = self.cols + round_up(2 + self.bias_cols, LANES)

    @staticmethod
    def fits(n):
        return n % KV == 0 and H % n == 0

    def slices(self, values):
        rows = values.shape[0]
        query = values[:, : H * HD].reshape(rows, self.n, self.q_cols)
        both = values[:, H * HD :].reshape(rows, 2, KV, 1, HD)
        both = jnp.broadcast_to(both, (rows, 2, KV, self.share, HD)).reshape(rows, 2, self.n, HD)
        return jnp.concatenate([query, both[:, 0], both[:, 1]], axis=2)

    def gather(self, attn_gain, mlp_gain, qkv_weight, qkv_bias, out_weight):
        rows, n, dp_n = self.rows, self.n, self.dp_n
        bias = pad_to(qkv_bias, 0, self.bias_cols * rows).reshape(self.bias_cols, rows)
        extra = jnp.concatenate([attn_gain[None], mlp_gain[None], bias], axis=0).T
        extra = pad_to(extra, 1, self.width - self.cols)
        extra = jnp.broadcast_to(extra[:, None], (rows, n, extra.shape[1]))
        pack = jnp.concatenate([self.slices(qkv_weight), extra], axis=2).transpose(1, 0, 2)
        pack = lax.all_to_all(pack, "ctx", 0, 0, tiled=True).reshape(n * rows, self.width)
        moves = [(b, (b % dp_n) * n + b // dp_n) for b in range(dp_n * n)]
        out_block = lax.ppermute(out_weight, ALL, moves)
        self.out_rows, self.out_cols = out_weight.shape
        self.extra_rows = self.out_rows * self.out_cols // self.width
        pack = jnp.concatenate([pack, out_block.reshape(self.extra_rows, self.width)], axis=0)
        whole = lax.all_gather(pack, "dp", axis=0, tiled=False)
        joint = whole[:, : n * rows].reshape(dp_n * n * rows, self.width)
        self.out_slice = whole[:, n * rows :].reshape(dp_n * self.out_rows, self.out_cols)
        self.joint = joint
        bias = joint[:, self.cols + 2 : self.cols + 2 + self.bias_cols]
        bias = bias.reshape(dp_n * n, rows, self.bias_cols).transpose(0, 2, 1)
        bias = bias.reshape(dp_n * n, self.bias_cols * rows)[:, : self.bias_rows].reshape(-1)
        self.bias_slice = jnp.concatenate(
            [lax.dynamic_slice(bias, (start,), (size,)) for start, size in self.places()]
        ).astype(F32)
        return joint[:, self.cols].astype(F32), joint[:, self.cols + 1].astype(F32)

    def places(self):
        me = self.peers.me
        group = me // self.share
        return (
            (me * self.q_cols, self.q_cols),
            (H * HD + group * HD, HD),
            (H * HD + KV * HD + group * HD, HD),
        )

    def forward(self, blocks, segment_ids, gain, before):
        peers, n = self.peers, self.n
        span = blocks[0].shape[0]
        length = n * span
        starts = [peers.source(step) * span for step in range(n)]
        index = jnp.concatenate([start + jnp.arange(span, dtype=jnp.int32) for start in starts])
        segments = jnp.concatenate(peers.spread(segment_ids), axis=1)[0]
        doc_start = jnp.sum((segments[None, :] < segments[:, None]).astype(jnp.int32), axis=1)
        self.cos_table, self.sin_table = rope_tables(index - doc_start)
        self.visible = (index[None, :] <= index[:, None]) & (
            segments[None, :] == segments[:, None]
        )
        self.scale = 1.0 / math.sqrt(HD)
        self.resid = jnp.concatenate(blocks).astype(F32)
        self.inv = inv_rms_of(self.resid)
        self.normed = (self.resid * self.inv * gain).astype(BF)
        projected = dot(self.normed, self.joint)[:, : self.cols] + self.bias_slice
        query_pre = projected[:, : self.q_cols].reshape(length, self.heads, HD)
        key_pre = projected[:, self.q_cols : self.q_cols + HD].reshape(length, 1, HD)
        self.values = projected[:, self.q_cols + HD : self.cols].astype(BF)
        self.query = rotate(query_pre, self.cos_table, self.sin_table).astype(BF)
        self.key = rotate(key_pre, self.cos_table, self.sin_table).astype(BF).reshape(length, HD)
        attended, self.log_total = attend(
            self.query, self.key, self.values, self.visible, self.scale
        )
        self.attended, before = lax.optimization_barrier((attended.astype(BF), before))
        flat = self.attended.reshape(length, self.q_cols)
        mixed = add_up(peers.deliver(dot(flat, self.out_slice).astype(BF)))
        return blocks[0].astype(F32) + mixed, before

    def backward(self, mid_grad, gain, gain_two_term, filled, joint_grad, finish):
        peers, n, rows, dp_n = self.peers, self.n, self.rows, self.dp_n
        span = mid_grad.shape[0]
        blocks, filled = lax.optimization_barrier((peers.spread(mid_grad.astype(BF)), filled))
        filled = peers.deliver(filled)
        low = jnp.concatenate(blocks)
        length = low.shape[0]
        attended_grad = dot_t(low, self.out_slice).astype(BF).reshape(length, self.heads, HD)
        out_term = t_dot(self.attended.reshape(length, self.q_cols), low)
        query_grad, key_grad, value_grad = attend_back(
            self.query,
            self.key,
            self.values,
            self.visible,
            self.attended,
            attended_grad,
            self.log_total,
            self.scale,
        )
        query_grad = rotate(query_grad, self.cos_table, -self.sin_table).reshape(length, -1)
        key_grad = rotate(key_grad[:, None], self.cos_table, -self.sin_table).reshape(length, HD)
        proj_grad = jnp.concatenate([query_grad, key_grad, value_grad], axis=1)
        bias_term = jnp.sum(proj_grad, axis=0)
        low_grad = pad_to(proj_grad.astype(BF), 1, self.width)
        partial = dot_t(low_grad, self.joint).astype(BF)
        partial, filled = lax.optimization_barrier((partial, filled))
        normed_shares = peers.deliver(partial)
        gain_term = jnp.sum(partial.astype(F32) * (self.resid * self.inv), axis=0)
        qkv_term = t_dot(self.normed, low_grad)
        bias = jnp.zeros((dp_n * n * self.bias_rows,), F32)
        first = 0
        for start, size in self.places():
            bias = lax.dynamic_update_slice(bias, bias_term[first : first + size], (start,))
            first += size
        bias = pad_to(bias.reshape(dp_n * n, self.bias_rows), 1, self.bias_cols * rows)
        bias = bias.reshape(dp_n * n, self.bias_cols, rows).transpose(1, 0, 2)
        extra = jnp.concatenate(
            [gain_term[None], gain_two_term[None], bias.reshape(self.bias_cols, -1)], axis=0
        ).T
        extra = jnp.pad(extra, ((0, 0), (self.cols, self.width - self.cols - extra.shape[1])))
        joint = (qkv_term + extra).astype(BF).reshape(dp_n, n * rows, self.width)
        out_term = out_term.astype(BF).reshape(dp_n, self.extra_rows, self.width)
        pack, joint_grad, normed_shares = lax.optimization_barrier(
            (jnp.concatenate([joint, out_term], axis=1), joint_grad, normed_shares)
        )
        mine = lax.psum_scatter(pack, "dp", scatter_dimension=0, tiled=False)
        own = slice(0, span)
        normed_grad = add_up(normed_shares)
        input_grad = mid_grad + norm_back(normed_grad, self.resid[own], self.inv[own], gain)
        mine, input_grad, output, finished = lax.optimization_barrier(
            (mine, input_grad, *finish(filled, joint_grad))
        )
        moves = [((b % dp_n) * n + b // dp_n, b) for b in range(dp_n * n)]
        out_grad = lax.ppermute(
            mine[n * rows :].reshape(self.out_rows, self.out_cols), ALL, moves
        ).astype(F32)
        parts = lax.all_to_all(
            mine[: n * rows].reshape(n, rows, self.width), "ctx", 0, 0, tiled=True
        ).astype(F32)
        query = parts[:, :, : self.q_cols].transpose(1, 0, 2).reshape(rows, -1)
        both = parts[:, :, self.q_cols : self.cols].reshape(KV, self.share, rows, 2, HD)
        both = jnp.sum(both, axis=1).transpose(1, 2, 0, 3).reshape(rows, -1)
        extra = jnp.sum(parts[:, :, self.cols :], axis=0)
        bias_grad = extra[:, 2 : 2 + self.bias_cols].T.reshape(-1)[: self.bias_rows]
        return (
            input_grad,
            extra[:, 0],
            jnp.concatenate([query, both], axis=1),
            bias_grad,
            out_grad,
            extra[:, 1],
        ), output, finished


class RowSplit:
    def __init__(self, peers):
        self.peers = peers

    def gather(self, attn_gain, mlp_gain, qkv_weight, qkv_bias, out_weight):
        gain_one, gain_two, self.qkv, bias, self.out = (
            lax.all_gather(part, ALL, axis=0, tiled=True)
            for part in (attn_gain, mlp_gain, qkv_weight, qkv_bias, out_weight)
        )
        self.bias = bias.astype(F32)
        return gain_one.astype(F32), gain_two.astype(F32)

    def forward(self, blocks, segment_ids, gain, before):
        own = blocks[0]
        span = own.shape[0]
        width = KV * HD
        segments = segment_ids[0]
        all_segments = lax.all_gather(segment_ids, "ctx", axis=1, tiled=True)[0]
        length = all_segments.shape[0]
        query_index = self.peers.me * span + jnp.arange(span, dtype=jnp.int32)
        key_index = jnp.arange(length, dtype=jnp.int32)
        doc_start = jnp.sum((all_segments[None] < segments[:, None]).astype(jnp.int32), axis=1)
        self.cos_table, self.sin_table = rope_tables(query_index - doc_start)
        self.visible = (key_index[None, :] <= query_index[:, None]) & (
            all_segments[None, :] == segments[:, None]
        )
        self.scale = 1.0 / math.sqrt(HD)
        self.resid = own.astype(F32)
        self.inv = inv_rms_of(self.resid)
        self.normed = (self.resid * self.inv * gain).astype(BF)
        projected = dot(self.normed, self.qkv) + self.bias
        query_pre = projected[:, : H * HD].reshape(span, H, HD)
        key_pre = projected[:, H * HD : H * HD + width].reshape(span, KV, HD)
        values = projected[:, H * HD + width :].astype(BF)
        self.query = rotate(query_pre, self.cos_table, self.sin_table).astype(BF)
        key_rot = rotate(key_pre, self.cos_table, self.sin_table).astype(BF).reshape(span, width)
        self.key, self.values = (
            lax.all_gather(part, "ctx", axis=0, tiled=True).reshape(length, KV, HD)
            for part in (key_rot, values)
        )
        pieces = [
            attend(
                self.query[:, self.part(group)],
                self.key[:, group],
                self.values[:, group],
                self.visible,
                self.scale,
            )
            for group in range(KV)
        ]
        self.attended = jnp.concatenate([piece[0] for piece in pieces], axis=1).astype(BF)
        self.log_totals = [piece[1] for piece in pieces]
        return self.resid + dot(self.attended.reshape(span, -1), self.out), before

    @staticmethod
    def part(group):
        return slice(group * (H // KV), (group + 1) * (H // KV))

    def backward(self, mid_grad, gain, gain_two_term, filled, joint_grad, finish):
        span = mid_grad.shape[0]
        low = mid_grad.astype(BF)
        attended_grad = dot_t(low, self.out).astype(BF).reshape(span, H, HD)
        grads = [
            attend_back(
                self.query[:, self.part(group)],
                self.key[:, group],
                self.values[:, group],
                self.visible,
                self.attended[:, self.part(group)],
                attended_grad[:, self.part(group)],
                self.log_totals[group],
                self.scale,
            )
            for group in range(KV)
        ]
        query_grad = jnp.concatenate([grad[0] for grad in grads], axis=1)
        key_grad, value_grad = (
            lax.psum_scatter(
                jnp.concatenate([grad[place] for grad in grads], axis=1).astype(BF),
                "ctx",
                scatter_dimension=0,
                tiled=True,
            ).astype(F32)
            for place in (1, 2)
        )
        query_grad = rotate(query_grad, self.cos_table, -self.sin_table).reshape(span, -1)
        key_grad = rotate(key_grad.reshape(span, KV, HD), self.cos_table, -self.sin_table)
        proj_grad = jnp.concatenate([query_grad, key_grad.reshape(span, -1), value_grad], axis=1)
        low_grad = proj_grad.astype(BF)
        normed_grad = dot_t(low_grad, self.qkv)
        input_grad = mid_grad + norm_back(normed_grad, self.resid, self.inv, gain)
        gain_term = jnp.sum(normed_grad * (self.resid * self.inv), axis=0)
        terms = (
            gain_term,
            t_dot(self.normed, low_grad).astype(BF),
            jnp.sum(proj_grad, axis=0),
            t_dot(self.attended.reshape(span, -1), low).astype(BF),
            gain_two_term,
        )
        grads = (input_grad,) + tuple(
            lax.psum_scatter(term, ALL, scatter_dimension=0, tiled=True).astype(F32)
            for term in terms
        )
        return grads, *finish(self.peers.deliver(filled), joint_grad)


def on_device(
    inputs,
    cotangent,
    segment_ids,
    attn_gain,
    qkv_weight,
    qkv_bias,
    out_weight,
    mlp_gain,
    gate_weight,
    up_weight,
    down_weight,
    *,
    dp_n,
    ctx_n,
):
    rows, hidden_width = gate_weight.shape
    n = ctx_n
    peers = Peers("ctx", n)
    if HeadSplit.fits(n):
        attention = HeadSplit(peers, dp_n, rows, qkv_bias.shape[0])
        blocks = peers.spread(inputs[0])
    else:
        attention = RowSplit(peers)
        blocks = [inputs[0]]
    gain_one, gain_two = attention.gather(attn_gain, mlp_gain, qkv_weight, qkv_bias, out_weight)

    unit = hidden_width // (dp_n * n)
    padded = round_up(unit, LANES // math.gcd(LANES, dp_n))
    wide = dp_n * padded

    def column_slices(weight):
        parts = pad_to(weight.reshape(rows, dp_n, n, unit), 3, padded)
        return parts.transpose(2, 0, 1, 3).reshape(n, rows, wide)

    def weight_columns(values):
        parts = values.reshape(n, rows, dp_n, padded)[..., :unit].transpose(1, 2, 0, 3)
        return parts.reshape(rows, hidden_width).astype(F32)

    joint = jnp.concatenate([column_slices(gate_weight), column_slices(up_weight)], axis=2)
    joint = peers.exchange(joint).reshape(n * rows, 2 * wide)
    gate_up = lax.all_gather(joint, "dp", axis=0, tiled=True)
    down = lax.all_gather(pad_to(down_weight, 0, padded), "dp", axis=0, tiled=True)

    blocks, own_cotangent = lax.optimization_barrier((blocks, cotangent[0]))
    grad_out = peers.spread(own_cotangent)
    resid_mid, grad_out = attention.forward(blocks, segment_ids, gain_one, grad_out)
    inv_two = inv_rms_of(resid_mid)
    normed_own = (resid_mid * inv_two * gain_two).astype(BF)
    normed = jnp.concatenate(peers.spread(normed_own))
    grad_out = jnp.concatenate(grad_out)
    pre = dot(normed, gate_up)
    gate_pre = pre[:, :wide]
    up_pre = pre[:, wide:]
    sigmoid_gate = jax.nn.sigmoid(gate_pre)
    silu_gate = gate_pre * sigmoid_gate
    hidden = (silu_gate * up_pre).astype(BF)
    down_term = t_dot(hidden, grad_out).astype(BF)
    down_term, grad_out = lax.optimization_barrier((down_term, grad_out))
    down_grad = lax.psum_scatter(down_term, "dp", scatter_dimension=0, tiled=True)
    hidden_grad = dot_t(grad_out, down)
    gate_grad = (
        hidden_grad * up_pre * sigmoid_gate * (1.0 + gate_pre * (1.0 - sigmoid_gate))
    ).astype(BF)
    up_grad = (hidden_grad * silu_gate).astype(BF)
    pre_grad = jnp.concatenate([gate_grad, up_grad], axis=1)
    shares = peers.deliver(dot_t(pre_grad, gate_up).astype(BF))
    joint_term = t_dot(normed, pre_grad).astype(BF)
    shares, joint_term = lax.optimization_barrier((shares, joint_term))
    joint_term, down_grad = lax.optimization_barrier((joint_term, down_grad))
    joint_grad = lax.psum_scatter(joint_term, "dp", scatter_dimension=0, tiled=True)

    normed_two_grad = add_up(shares)
    gain_two_term = jnp.sum(normed_two_grad * (resid_mid * inv_two), axis=0)
    mid_grad = cotangent[0].astype(F32) + norm_back(normed_two_grad, resid_mid, inv_two, gain_two)

    def finish(output_shares, joint_grad):
        output = resid_mid + add_up(output_shares)
        parts = peers.exchange(joint_grad.reshape(n, rows, 2 * wide))
        grads = (weight_columns(parts[:, :, :wide]), weight_columns(parts[:, :, wide:]))
        return output.astype(BF), grads

    grads, output, (gate_weight_grad, up_weight_grad) = attention.backward(
        mid_grad, gain_one, gain_two_term, dot(hidden, down).astype(BF), joint_grad, finish
    )
    input_grad, attn_gain_grad, qkv_weight_grad, qkv_bias_grad, out_weight_grad, mlp_gain_grad = (
        grads
    )
    return (
        output[None],
        input_grad[None],
        attn_gain_grad,
        qkv_weight_grad,
        qkv_bias_grad,
        out_weight_grad,
        mlp_gain_grad,
        gate_weight_grad,
        up_weight_grad,
        down_grad[:unit].astype(F32),
    )


def solution(mesh):
    body = functools.partial(on_device, dp_n=mesh.shape["dp"], ctx_n=mesh.shape["ctx"])
    return jax.shard_map(
        body,
        mesh=mesh,
        in_specs=(
            P("dp", "ctx", None),
            P("dp", "ctx", None),
            P("dp", "ctx"),
            P(ALL),
            P(ALL, None),
            P(ALL),
            P(ALL, None),
            P(ALL),
            P(ALL, None),
            P(ALL, None),
            P(ALL, None),
        ),
        out_specs=(
            P("dp", "ctx", None),
            P("dp", "ctx", None),
            P(ALL),
            P(ALL, None),
            P(ALL),
            P(ALL, None),
            P(ALL),
            P(ALL, None),
            P(ALL, None),
            P(ALL, None),
        ),
        check_vma=False,
    )
```

```python
import functools
import math

import jax
import jax.numpy as jnp
from jax import lax
from jax.sharding import PartitionSpec as P

H = 12
KV = 2
HD = 128
LANES = 128


EPS = 1e-06
THETA = 1000000.0
MASKED = -1e30
BF = jnp.bfloat16
F32 = jnp.float32
ALL = ("dp", "ctx")


def rope_tables(positions):
    half_dim = jnp.arange(0, HD, 2).astype(F32) / HD
    inverse = THETA ** (-half_dim)
    angles = positions.astype(F32)[:, None] * inverse[None, :]
    angles = jnp.concatenate([angles, angles], axis=1)
    return (jnp.cos(angles), jnp.sin(angles))


def rotate(values, cos_table, sin_table):
    half_dim = values.shape[-1] // 2
    turned = jnp.concatenate([-values[..., half_dim:], values[..., :half_dim]], axis=-1)
    return values * cos_table[:, None, :] + turned * sin_table[:, None, :]


def inv_rms_of(values):
    return lax.rsqrt(jnp.mean(values * values, axis=-1, keepdims=True) + EPS)


def norm_back(normed_grad, values, inv_rms, gain):
    normed = values * inv_rms
    scaled_grad = normed_grad * gain
    return inv_rms * (scaled_grad - normed * jnp.mean(scaled_grad * normed, axis=-1, keepdims=True))


def dot(a, b):
    return jnp.dot(a, b, preferred_element_type=F32)


def dot_t(a, b):
    return lax.dot_general(a, b, (((1,), (1,)), ((), ())), preferred_element_type=F32)


def t_dot(a, b):
    return lax.dot_general(a, b, (((0,), (0,)), ((), ())), preferred_element_type=F32)


def attend(queries, key_rows, value_rows, visible, scale_factor):
    scores = jnp.einsum("tjd,nd->jtn", queries, key_rows, preferred_element_type=F32) * scale_factor
    scores = jnp.where(visible[None], scores, MASKED)
    row_max = jnp.max(scores, axis=-1, keepdims=True)
    row_sum = jnp.sum(jnp.exp(scores - row_max), axis=-1, keepdims=True)
    log_total = row_max + jnp.log(row_sum)
    weights = jnp.exp(scores - log_total).astype(BF)
    mixed = jnp.einsum("jtn,nd->tjd", weights, value_rows, preferred_element_type=F32)
    return mixed, log_total


def attend_back(
    queries, key_rows, value_rows, visible, attended, attended_grad, log_total, scale_factor
):
    scores = jnp.einsum("tjd,nd->jtn", queries, key_rows, preferred_element_type=F32) * scale_factor
    scores = jnp.where(visible[None], scores, MASKED)
    probs_full = jnp.exp(scores - log_total)
    probs_low = probs_full.astype(BF)
    value_grad = jnp.einsum("jtn,tjd->nd", probs_low, attended_grad, preferred_element_type=F32)
    prob_grad = jnp.einsum("tjd,nd->jtn", attended_grad, value_rows, preferred_element_type=F32)
    row_dot = jnp.sum(attended_grad.astype(F32) * attended.astype(F32), axis=-1).T
    score_grad = (probs_full * (prob_grad - row_dot[..., None]) * scale_factor).astype(BF)
    query_grad = jnp.einsum("jtn,nd->tjd", score_grad, key_rows, preferred_element_type=F32)
    key_grad = jnp.einsum("jtn,tjd->nd", score_grad, queries, preferred_element_type=F32)
    return query_grad, key_grad, value_grad


class Peers:
    def __init__(self, axis, size):
        self.axis = axis
        self.size = size
        self.paired = size & (size - 1) == 0
        self.me = lax.axis_index(axis)

    def to(self, index, step):
        return index ^ step if self.paired else (index + step) % self.size

    def source(self, step):
        return self.me ^ step if self.paired else (self.me - step + self.size) % self.size

    def spread(self, own):
        blocks = [own]
        for step in range(1, self.size):
            pairs = [(i, self.to(i, step)) for i in range(self.size)]
            blocks.append(lax.ppermute(own, self.axis, pairs))
        return blocks

    def exchange(self, parts):
        received = []
        for step in range(1, self.size):
            pairs = [(self.to(i, step), i) for i in range(self.size)]
            block = lax.dynamic_index_in_dim(parts, self.source(step), 0)
            received.append(lax.ppermute(block, self.axis, pairs))
        parts, received = lax.optimization_barrier((parts, received))
        for step, block in enumerate(received, 1):
            target = self.source(step) if self.paired else (self.me + step) % self.size
            parts = lax.dynamic_update_slice_in_dim(parts, block, target, 0)
        return parts

    def deliver(self, partial):
        span = partial.shape[0] // self.size
        received = [partial[:span]]
        for step in range(self.size - 1, 0, -1):
            pairs = [(self.to(i, step), i) for i in range(self.size)]
            share = partial[step * span : (step + 1) * span]
            received.append(lax.ppermute(share, self.axis, pairs))
        return received


def add_up(shares):
    return sum(share.astype(F32) for share in shares[1:]) + shares[0].astype(F32)


def pad_to(values, axis, size):
    widths = [(0, 0)] * values.ndim
    widths[axis] = (0, size - values.shape[axis])
    return jnp.pad(values, widths)


def round_up(value, unit):
    return -(-value // unit) * unit


class HeadSplit:
    def __init__(self, peers, dp_n, rows, bias_rows):
        self.peers = peers
        self.n = peers.size
        self.dp_n = dp_n
        self.rows = rows
        self.bias_rows = bias_rows
        self.share = self.n // KV
        self.heads = H // self.n
        self.q_cols = self.heads * HD
        self.cols = self.q_cols + 2 * HD
        self.bias_cols = -(-bias_rows // rows)
        self.width = self.cols + round_up(2 + self.bias_cols, LANES)

    @staticmethod
    def fits(n, dp_n):
        return n % KV == 0 and H % n == 0 and dp_n % n == 0

    def slices(self, values):
        rows = values.shape[0]
        query = values[:, : H * HD].reshape(rows, self.n, self.q_cols)
        both = values[:, H * HD :].reshape(rows, 2, KV, 1, HD)
        both = jnp.broadcast_to(both, (rows, 2, KV, self.share, HD)).reshape(rows, 2, self.n, HD)
        return jnp.concatenate([query, both[:, 0], both[:, 1]], axis=2)

    def gather(self, attn_gain, mlp_gain, qkv_weight, qkv_bias, out_weight):
        rows, n, dp_n = self.rows, self.n, self.dp_n
        bias = pad_to(qkv_bias, 0, self.bias_cols * rows).reshape(self.bias_cols, rows)
        extra = jnp.concatenate([attn_gain[None], mlp_gain[None], bias], axis=0).T
        extra = pad_to(extra, 1, self.width - self.cols)
        own = jnp.concatenate([qkv_weight, extra, out_weight], axis=1)
        whole = lax.all_gather(own, "dp", axis=0, tiled=False)
        qkv_cols, out_first = qkv_weight.shape[1], qkv_weight.shape[1] + extra.shape[1]
        qkv = whole[:, :, :qkv_cols].reshape(dp_n * rows, qkv_cols)
        extra = whole[:, :, qkv_cols:out_first].reshape(dp_n * rows, 1, -1)
        extra = jnp.broadcast_to(extra, (dp_n * rows, n, extra.shape[2]))
        parts = jnp.concatenate([self.slices(qkv), extra], axis=2).transpose(1, 0, 2)
        blocks = whole[:, :, out_first:]
        parts, blocks = lax.optimization_barrier((self.peers.exchange(parts), blocks))
        parts = parts.reshape(n, dp_n, rows, self.width)
        joint = parts.transpose(1, 0, 2, 3).reshape(dp_n * n * rows, self.width)
        self.out_rows, self.out_cols = out_weight.shape
        self.extra_rows = self.out_rows * self.out_cols // self.width
        run = dp_n // n
        blocks = blocks.reshape(n, run, rows, self.out_cols)
        blocks = self.peers.exchange(blocks).transpose(1, 0, 2, 3)
        self.out_slice = blocks.reshape(dp_n * rows, self.out_cols)
        self.joint = joint
        bias = joint[:, self.cols + 2 : self.cols + 2 + self.bias_cols]
        bias = bias.reshape(dp_n * n, rows, self.bias_cols).transpose(0, 2, 1)
        bias = bias.reshape(dp_n * n, self.bias_cols * rows)[:, : self.bias_rows].reshape(-1)
        self.bias_slice = jnp.concatenate(
            [lax.dynamic_slice(bias, (start,), (size,)) for start, size in self.places()]
        ).astype(F32)
        return joint[:, self.cols].astype(F32), joint[:, self.cols + 1].astype(F32)

    def hold(self, values):
        self.joint, values = lax.optimization_barrier((self.joint, values))
        return values

    def places(self):
        me = self.peers.me
        group = me // self.share
        return (
            (me * self.q_cols, self.q_cols),
            (H * HD + group * HD, HD),
            (H * HD + KV * HD + group * HD, HD),
        )

    def forward(self, blocks, segment_ids, gain, before):
        peers, n = self.peers, self.n
        span = blocks[0].shape[0]
        length = n * span
        starts = [peers.source(step) * span for step in range(n)]
        index = jnp.concatenate([start + jnp.arange(span, dtype=jnp.int32) for start in starts])
        segments = jnp.concatenate(peers.spread(segment_ids), axis=1)[0]
        doc_start = jnp.sum((segments[None, :] < segments[:, None]).astype(jnp.int32), axis=1)
        self.cos_table, self.sin_table = rope_tables(index - doc_start)
        self.visible = (index[None, :] <= index[:, None]) & (
            segments[None, :] == segments[:, None]
        )
        self.scale = 1.0 / math.sqrt(HD)
        self.resid = jnp.concatenate(blocks).astype(F32)
        self.inv = inv_rms_of(self.resid)
        self.normed = (self.resid * self.inv * gain).astype(BF)
        projected = dot(self.normed, self.joint)[:, : self.cols] + self.bias_slice
        query_pre = projected[:, : self.q_cols].reshape(length, self.heads, HD)
        key_pre = projected[:, self.q_cols : self.q_cols + HD].reshape(length, 1, HD)
        self.values = projected[:, self.q_cols + HD : self.cols].astype(BF)
        self.query = rotate(query_pre, self.cos_table, self.sin_table).astype(BF)
        self.key = rotate(key_pre, self.cos_table, self.sin_table).astype(BF).reshape(length, HD)
        attended, self.log_total = attend(
            self.query, self.key, self.values, self.visible, self.scale
        )
        self.attended, before = lax.optimization_barrier((attended.astype(BF), before))
        flat = self.attended.reshape(length, self.q_cols)
        mixed = add_up(peers.deliver(dot(flat, self.out_slice).astype(BF)))
        return blocks[0].astype(F32) + mixed, before

    def backward(self, mid_grad, gain, gain_two_term, filled, joint_grad, finish):
        peers, n, rows, dp_n = self.peers, self.n, self.rows, self.dp_n
        span = mid_grad.shape[0]
        blocks, filled = lax.optimization_barrier((peers.spread(mid_grad.astype(BF)), filled))
        filled = peers.deliver(filled)
        low = jnp.concatenate(blocks)
        length = low.shape[0]
        attended_grad = dot_t(low, self.out_slice).astype(BF).reshape(length, self.heads, HD)
        out_term = t_dot(self.attended.reshape(length, self.q_cols), low)
        query_grad, key_grad, value_grad = attend_back(
            self.query,
            self.key,
            self.values,
            self.visible,
            self.attended,
            attended_grad,
            self.log_total,
            self.scale,
        )
        query_grad = rotate(query_grad, self.cos_table, -self.sin_table).reshape(length, -1)
        key_grad = rotate(key_grad[:, None], self.cos_table, -self.sin_table).reshape(length, HD)
        proj_grad = jnp.concatenate([query_grad, key_grad, value_grad], axis=1)
        bias_term = jnp.sum(proj_grad, axis=0)
        low_grad = pad_to(proj_grad.astype(BF), 1, self.width)
        partial = dot_t(low_grad, self.joint).astype(BF)
        partial, filled = lax.optimization_barrier((partial, filled))
        normed_shares = peers.deliver(partial)
        gain_term = jnp.sum(partial.astype(F32) * (self.resid * self.inv), axis=0)
        qkv_term = t_dot(self.normed, low_grad)
        bias = jnp.zeros((dp_n * n * self.bias_rows,), F32)
        first = 0
        for start, size in self.places():
            bias = lax.dynamic_update_slice(bias, bias_term[first : first + size], (start,))
            first += size
        bias = pad_to(bias.reshape(dp_n * n, self.bias_rows), 1, self.bias_cols * rows)
        bias = bias.reshape(dp_n * n, self.bias_cols, rows).transpose(1, 0, 2)
        extra = jnp.concatenate(
            [gain_term[None], gain_two_term[None], bias.reshape(self.bias_cols, -1)], axis=0
        ).T
        extra = jnp.pad(extra, ((0, 0), (self.cols, self.width - self.cols - extra.shape[1])))
        joint = (qkv_term + extra).astype(BF).reshape(dp_n, n * rows, self.width)
        out_term = out_term.astype(BF).reshape(dp_n, self.extra_rows, self.width)
        pack, joint_grad, normed_shares = lax.optimization_barrier(
            (jnp.concatenate([joint, out_term], axis=1), joint_grad, normed_shares)
        )
        mine = lax.psum_scatter(pack, "dp", scatter_dimension=0, tiled=False)
        own = slice(0, span)
        normed_grad = add_up(normed_shares)
        input_grad = mid_grad + norm_back(normed_grad, self.resid[own], self.inv[own], gain)
        mine, input_grad, output, finished = lax.optimization_barrier(
            (mine, input_grad, *finish(filled, joint_grad))
        )
        moves = [((b % dp_n) * n + b // dp_n, b) for b in range(dp_n * n)]
        out_grad = lax.ppermute(
            mine[n * rows :].reshape(self.out_rows, self.out_cols), ALL, moves
        ).astype(F32)
        parts = lax.all_to_all(
            mine[: n * rows].reshape(n, rows, self.width), "ctx", 0, 0, tiled=True
        ).astype(F32)
        query = parts[:, :, : self.q_cols].transpose(1, 0, 2).reshape(rows, -1)
        both = parts[:, :, self.q_cols : self.cols].reshape(KV, self.share, rows, 2, HD)
        both = jnp.sum(both, axis=1).transpose(1, 2, 0, 3).reshape(rows, -1)
        extra = jnp.sum(parts[:, :, self.cols :], axis=0)
        bias_grad = extra[:, 2 : 2 + self.bias_cols].T.reshape(-1)[: self.bias_rows]
        return (
            input_grad,
            extra[:, 0],
            jnp.concatenate([query, both], axis=1),
            bias_grad,
            out_grad,
            extra[:, 1],
        ), output, finished


class RowSplit:
    def __init__(self, peers):
        self.peers = peers

    def gather(self, attn_gain, mlp_gain, qkv_weight, qkv_bias, out_weight):
        gain_one, gain_two, self.qkv, bias, self.out = (
            lax.all_gather(part, ALL, axis=0, tiled=True)
            for part in (attn_gain, mlp_gain, qkv_weight, qkv_bias, out_weight)
        )
        self.bias = bias.astype(F32)
        return gain_one.astype(F32), gain_two.astype(F32)

    def forward(self, blocks, segment_ids, gain, before):
        own = blocks[0]
        span = own.shape[0]
        width = KV * HD
        segments = segment_ids[0]
        all_segments = lax.all_gather(segment_ids, "ctx", axis=1, tiled=True)[0]
        length = all_segments.shape[0]
        query_index = self.peers.me * span + jnp.arange(span, dtype=jnp.int32)
        key_index = jnp.arange(length, dtype=jnp.int32)
        doc_start = jnp.sum((all_segments[None] < segments[:, None]).astype(jnp.int32), axis=1)
        self.cos_table, self.sin_table = rope_tables(query_index - doc_start)
        self.visible = (key_index[None, :] <= query_index[:, None]) & (
            all_segments[None, :] == segments[:, None]
        )
        self.scale = 1.0 / math.sqrt(HD)
        self.resid = own.astype(F32)
        self.inv = inv_rms_of(self.resid)
        self.normed = (self.resid * self.inv * gain).astype(BF)
        projected = dot(self.normed, self.qkv) + self.bias
        query_pre = projected[:, : H * HD].reshape(span, H, HD)
        key_pre = projected[:, H * HD : H * HD + width].reshape(span, KV, HD)
        values = projected[:, H * HD + width :].astype(BF)
        self.query = rotate(query_pre, self.cos_table, self.sin_table).astype(BF)
        key_rot = rotate(key_pre, self.cos_table, self.sin_table).astype(BF).reshape(span, width)
        self.key, self.values = (
            lax.all_gather(part, "ctx", axis=0, tiled=True).reshape(length, KV, HD)
            for part in (key_rot, values)
        )
        pieces = [
            attend(
                self.query[:, self.part(group)],
                self.key[:, group],
                self.values[:, group],
                self.visible,
                self.scale,
            )
            for group in range(KV)
        ]
        self.attended = jnp.concatenate([piece[0] for piece in pieces], axis=1).astype(BF)
        self.log_totals = [piece[1] for piece in pieces]
        return self.resid + dot(self.attended.reshape(span, -1), self.out), before

    def hold(self, values):
        return values

    @staticmethod
    def part(group):
        return slice(group * (H // KV), (group + 1) * (H // KV))

    def backward(self, mid_grad, gain, gain_two_term, filled, joint_grad, finish):
        span = mid_grad.shape[0]
        low = mid_grad.astype(BF)
        attended_grad = dot_t(low, self.out).astype(BF).reshape(span, H, HD)
        grads = [
            attend_back(
                self.query[:, self.part(group)],
                self.key[:, group],
                self.values[:, group],
                self.visible,
                self.attended[:, self.part(group)],
                attended_grad[:, self.part(group)],
                self.log_totals[group],
                self.scale,
            )
            for group in range(KV)
        ]
        query_grad = jnp.concatenate([grad[0] for grad in grads], axis=1)
        key_grad, value_grad = (
            lax.psum_scatter(
                jnp.concatenate([grad[place] for grad in grads], axis=1).astype(BF),
                "ctx",
                scatter_dimension=0,
                tiled=True,
            ).astype(F32)
            for place in (1, 2)
        )
        query_grad = rotate(query_grad, self.cos_table, -self.sin_table).reshape(span, -1)
        key_grad = rotate(key_grad.reshape(span, KV, HD), self.cos_table, -self.sin_table)
        proj_grad = jnp.concatenate([query_grad, key_grad.reshape(span, -1), value_grad], axis=1)
        low_grad = proj_grad.astype(BF)
        normed_grad = dot_t(low_grad, self.qkv)
        input_grad = mid_grad + norm_back(normed_grad, self.resid, self.inv, gain)
        gain_term = jnp.sum(normed_grad * (self.resid * self.inv), axis=0)
        terms = (
            gain_term,
            t_dot(self.normed, low_grad).astype(BF),
            jnp.sum(proj_grad, axis=0),
            t_dot(self.attended.reshape(span, -1), low).astype(BF),
            gain_two_term,
        )
        grads = (input_grad,) + tuple(
            lax.psum_scatter(term, ALL, scatter_dimension=0, tiled=True).astype(F32)
            for term in terms
        )
        return grads, *finish(self.peers.deliver(filled), joint_grad)


def on_device(
    inputs,
    cotangent,
    segment_ids,
    attn_gain,
    qkv_weight,
    qkv_bias,
    out_weight,
    mlp_gain,
    gate_weight,
    up_weight,
    down_weight,
    *,
    dp_n,
    ctx_n,
):
    rows, hidden_width = gate_weight.shape
    n = ctx_n
    peers = Peers("ctx", n)
    if HeadSplit.fits(n, dp_n) and out_weight.shape[0] == rows:
        attention = HeadSplit(peers, dp_n, rows, qkv_bias.shape[0])
        blocks = peers.spread(inputs[0])
    else:
        attention = RowSplit(peers)
        blocks = [inputs[0]]
    gain_one, gain_two = attention.gather(attn_gain, mlp_gain, qkv_weight, qkv_bias, out_weight)

    unit = hidden_width // (dp_n * n)
    padded = round_up(unit, LANES // math.gcd(LANES, dp_n))
    wide = dp_n * padded

    def column_slices(weight):
        parts = pad_to(weight.reshape(rows, dp_n, n, unit), 3, padded)
        return parts.transpose(2, 0, 1, 3).reshape(n, rows, wide)

    def weight_columns(values):
        parts = values.reshape(n, rows, dp_n, padded)[..., :unit].transpose(1, 2, 0, 3)
        return parts.reshape(rows, hidden_width).astype(F32)

    joint = jnp.concatenate([column_slices(gate_weight), column_slices(up_weight)], axis=2)
    joint = peers.exchange(joint).reshape(n * rows, 2 * wide)
    gate_up = lax.all_gather(joint, "dp", axis=0, tiled=True)
    down = lax.all_gather(pad_to(down_weight, 0, padded), "dp", axis=0, tiled=True)

    blocks, own_cotangent = lax.optimization_barrier((blocks, cotangent[0]))
    grad_out = peers.spread(attention.hold(own_cotangent))
    resid_mid, grad_out = attention.forward(blocks, segment_ids, gain_one, grad_out)
    inv_two = inv_rms_of(resid_mid)
    normed_own = (resid_mid * inv_two * gain_two).astype(BF)
    normed = jnp.concatenate(peers.spread(normed_own))
    grad_out = jnp.concatenate(grad_out)
    pre = dot(normed, gate_up)
    gate_pre = pre[:, :wide]
    up_pre = pre[:, wide:]
    sigmoid_gate = jax.nn.sigmoid(gate_pre)
    silu_gate = gate_pre * sigmoid_gate
    hidden = (silu_gate * up_pre).astype(BF)
    down_term = t_dot(hidden, grad_out).astype(BF)
    down_term, grad_out = lax.optimization_barrier((down_term, grad_out))
    down_grad = lax.psum_scatter(down_term, "dp", scatter_dimension=0, tiled=True)
    hidden_grad = dot_t(grad_out, down)
    gate_grad = (
        hidden_grad * up_pre * sigmoid_gate * (1.0 + gate_pre * (1.0 - sigmoid_gate))
    ).astype(BF)
    up_grad = (hidden_grad * silu_gate).astype(BF)
    pre_grad = jnp.concatenate([gate_grad, up_grad], axis=1)
    shares = peers.deliver(dot_t(pre_grad, gate_up).astype(BF))
    joint_term = t_dot(normed, pre_grad).astype(BF)
    shares, joint_term = lax.optimization_barrier((shares, joint_term))
    joint_term, down_grad = lax.optimization_barrier((joint_term, down_grad))
    joint_grad = lax.psum_scatter(joint_term, "dp", scatter_dimension=0, tiled=True)

    normed_two_grad = add_up(shares)
    gain_two_term = jnp.sum(normed_two_grad * (resid_mid * inv_two), axis=0)
    mid_grad = cotangent[0].astype(F32) + norm_back(normed_two_grad, resid_mid, inv_two, gain_two)

    def finish(output_shares, joint_grad):
        output = resid_mid + add_up(output_shares)
        parts = peers.exchange(joint_grad.reshape(n, rows, 2 * wide))
        grads = (weight_columns(parts[:, :, :wide]), weight_columns(parts[:, :, wide:]))
        return output.astype(BF), grads

    grads, output, (gate_weight_grad, up_weight_grad) = attention.backward(
        mid_grad, gain_one, gain_two_term, dot(hidden, down).astype(BF), joint_grad, finish
    )
    input_grad, attn_gain_grad, qkv_weight_grad, qkv_bias_grad, out_weight_grad, mlp_gain_grad = (
        grads
    )
    return (
        output[None],
        input_grad[None],
        attn_gain_grad,
        qkv_weight_grad,
        qkv_bias_grad,
        out_weight_grad,
        mlp_gain_grad,
        gate_weight_grad,
        up_weight_grad,
        down_grad[:unit].astype(F32),
    )


def solution(mesh):
    body = functools.partial(on_device, dp_n=mesh.shape["dp"], ctx_n=mesh.shape["ctx"])
    return jax.shard_map(
        body,
        mesh=mesh,
        in_specs=(
            P("dp", "ctx", None),
            P("dp", "ctx", None),
            P("dp", "ctx"),
            P(ALL),
            P(ALL, None),
            P(ALL),
            P(ALL, None),
            P(ALL),
            P(ALL, None),
            P(ALL, None),
            P(ALL, None),
        ),
        out_specs=(
            P("dp", "ctx", None),
            P("dp", "ctx", None),
            P(ALL),
            P(ALL, None),
            P(ALL),
            P(ALL, None),
            P(ALL),
            P(ALL, None),
            P(ALL, None),
            P(ALL, None),
        ),
        check_vma=False,
    )
```

```python
import functools
import math

import jax
import jax.numpy as jnp
from jax import lax
from jax.sharding import PartitionSpec as P

H = 12
KV = 2
HD = 128
LANES = 128


EPS = 1e-06
THETA = 1000000.0
MASKED = -1e30
BF = jnp.bfloat16
F32 = jnp.float32
ALL = ("dp", "ctx")


def rope_tables(positions):
    half_dim = jnp.arange(0, HD, 2).astype(F32) / HD
    inverse = THETA ** (-half_dim)
    angles = positions.astype(F32)[:, None] * inverse[None, :]
    angles = jnp.concatenate([angles, angles], axis=1)
    return (jnp.cos(angles), jnp.sin(angles))


def rotate(values, cos_table, sin_table):
    half_dim = values.shape[-1] // 2
    turned = jnp.concatenate([-values[..., half_dim:], values[..., :half_dim]], axis=-1)
    return values * cos_table[:, None, :] + turned * sin_table[:, None, :]


def inv_rms_of(values):
    return lax.rsqrt(jnp.mean(values * values, axis=-1, keepdims=True) + EPS)


def norm_back(normed_grad, values, inv_rms, gain):
    normed = values * inv_rms
    scaled_grad = normed_grad * gain
    return inv_rms * (scaled_grad - normed * jnp.mean(scaled_grad * normed, axis=-1, keepdims=True))


def dot(a, b):
    return jnp.dot(a, b, preferred_element_type=F32)


def dot_t(a, b):
    return lax.dot_general(a, b, (((1,), (1,)), ((), ())), preferred_element_type=F32)


def t_dot(a, b):
    return lax.dot_general(a, b, (((0,), (0,)), ((), ())), preferred_element_type=F32)


def attend(queries, key_rows, value_rows, visible, scale_factor):
    scores = jnp.einsum("tjd,nd->jtn", queries, key_rows, preferred_element_type=F32) * scale_factor
    scores = jnp.where(visible[None], scores, MASKED)
    row_max = jnp.max(scores, axis=-1, keepdims=True)
    row_sum = jnp.sum(jnp.exp(scores - row_max), axis=-1, keepdims=True)
    log_total = row_max + jnp.log(row_sum)
    weights = jnp.exp(scores - log_total).astype(BF)
    mixed = jnp.einsum("jtn,nd->tjd", weights, value_rows, preferred_element_type=F32)
    return mixed, log_total


def attend_back(
    queries, key_rows, value_rows, visible, attended, attended_grad, log_total, scale_factor
):
    scores = jnp.einsum("tjd,nd->jtn", queries, key_rows, preferred_element_type=F32) * scale_factor
    scores = jnp.where(visible[None], scores, MASKED)
    probs_full = jnp.exp(scores - log_total)
    probs_low = probs_full.astype(BF)
    value_grad = jnp.einsum("jtn,tjd->nd", probs_low, attended_grad, preferred_element_type=F32)
    prob_grad = jnp.einsum("tjd,nd->jtn", attended_grad, value_rows, preferred_element_type=F32)
    row_dot = jnp.sum(attended_grad.astype(F32) * attended.astype(F32), axis=-1).T
    score_grad = (probs_full * (prob_grad - row_dot[..., None]) * scale_factor).astype(BF)
    query_grad = jnp.einsum("jtn,nd->tjd", score_grad, key_rows, preferred_element_type=F32)
    key_grad = jnp.einsum("jtn,tjd->nd", score_grad, queries, preferred_element_type=F32)
    return query_grad, key_grad, value_grad


class Peers:
    def __init__(self, axis, size):
        self.axis = axis
        self.size = size
        self.paired = size & (size - 1) == 0
        self.me = lax.axis_index(axis)

    def to(self, index, step):
        return index ^ step if self.paired else (index + step) % self.size

    def source(self, step):
        return self.me ^ step if self.paired else (self.me - step + self.size) % self.size

    def spread(self, own):
        blocks = [own]
        for step in range(1, self.size):
            pairs = [(i, self.to(i, step)) for i in range(self.size)]
            blocks.append(lax.ppermute(own, self.axis, pairs))
        return blocks

    def exchange(self, parts):
        received = []
        for step in range(1, self.size):
            pairs = [(self.to(i, step), i) for i in range(self.size)]
            block = lax.dynamic_index_in_dim(parts, self.source(step), 0)
            received.append(lax.ppermute(block, self.axis, pairs))
        parts, received = lax.optimization_barrier((parts, received))
        for step, block in enumerate(received, 1):
            target = self.source(step) if self.paired else (self.me + step) % self.size
            parts = lax.dynamic_update_slice_in_dim(parts, block, target, 0)
        return parts

    def deliver(self, partial):
        span = partial.shape[0] // self.size
        received = [partial[:span]]
        for step in range(self.size - 1, 0, -1):
            pairs = [(self.to(i, step), i) for i in range(self.size)]
            share = partial[step * span : (step + 1) * span]
            received.append(lax.ppermute(share, self.axis, pairs))
        return received


def add_up(shares):
    return sum(share.astype(F32) for share in shares[1:]) + shares[0].astype(F32)


def pad_to(values, axis, size):
    widths = [(0, 0)] * values.ndim
    widths[axis] = (0, size - values.shape[axis])
    return jnp.pad(values, widths)


def round_up(value, unit):
    return -(-value // unit) * unit


class HeadSplit:
    def __init__(self, peers, dp_n, rows, bias_rows):
        self.peers = peers
        self.n = peers.size
        self.dp_n = dp_n
        self.rows = rows
        self.bias_rows = bias_rows
        self.share = self.n // KV
        self.heads = H // self.n
        self.q_cols = self.heads * HD
        self.cols = self.q_cols + 2 * HD
        self.bias_cols = -(-bias_rows // rows)
        self.width = self.cols + round_up(2 + self.bias_cols, LANES)

    @staticmethod
    def fits(n, dp_n):
        return n % KV == 0 and H % n == 0 and dp_n % n == 0

    def slices(self, values):
        rows = values.shape[0]
        query = values[:, : H * HD].reshape(rows, self.n, self.q_cols)
        both = values[:, H * HD :].reshape(rows, 2, KV, 1, HD)
        both = jnp.broadcast_to(both, (rows, 2, KV, self.share, HD)).reshape(rows, 2, self.n, HD)
        return jnp.concatenate([query, both[:, 0], both[:, 1]], axis=2)

    def gather(self, attn_gain, mlp_gain, qkv_weight, qkv_bias, out_weight):
        rows, n, dp_n = self.rows, self.n, self.dp_n
        bias = pad_to(qkv_bias, 0, self.bias_cols * rows).reshape(self.bias_cols, rows)
        extra = jnp.concatenate([attn_gain[None], mlp_gain[None], bias], axis=0).T
        extra = pad_to(extra, 1, self.width - self.cols)
        own = jnp.concatenate([qkv_weight, extra, out_weight], axis=1)
        whole = lax.all_gather(own, "dp", axis=0, tiled=False)
        qkv_cols, out_first = qkv_weight.shape[1], qkv_weight.shape[1] + extra.shape[1]
        qkv = whole[:, :, :qkv_cols].reshape(dp_n * rows, qkv_cols)
        extra = whole[:, :, qkv_cols:out_first].reshape(dp_n * rows, 1, -1)
        extra = jnp.broadcast_to(extra, (dp_n * rows, n, extra.shape[2]))
        parts = jnp.concatenate([self.slices(qkv), extra], axis=2).transpose(1, 0, 2)
        blocks = whole[:, :, out_first:]
        parts, blocks = lax.optimization_barrier((self.peers.exchange(parts), blocks))
        parts = parts.reshape(n, dp_n, rows, self.width)
        joint = parts.transpose(1, 0, 2, 3).reshape(dp_n * n * rows, self.width)
        self.out_rows, self.out_cols = out_weight.shape
        self.extra_rows = self.out_rows * self.out_cols // self.width
        run = dp_n // n
        blocks = blocks.reshape(n, run, rows, self.out_cols)
        blocks = self.peers.exchange(blocks).transpose(1, 0, 2, 3)
        self.out_slice = blocks.reshape(dp_n * rows, self.out_cols)
        self.joint = joint
        bias = joint[:, self.cols + 2 : self.cols + 2 + self.bias_cols]
        bias = bias.reshape(dp_n * n, rows, self.bias_cols).transpose(0, 2, 1)
        bias = bias.reshape(dp_n * n, self.bias_cols * rows)[:, : self.bias_rows].reshape(-1)
        self.bias_slice = jnp.concatenate(
            [lax.dynamic_slice(bias, (start,), (size,)) for start, size in self.places()]
        ).astype(F32)
        return joint[:, self.cols].astype(F32), joint[:, self.cols + 1].astype(F32)

    def places(self):
        me = self.peers.me
        group = me // self.share
        return (
            (me * self.q_cols, self.q_cols),
            (H * HD + group * HD, HD),
            (H * HD + KV * HD + group * HD, HD),
        )

    def forward(self, blocks, segment_ids, gain):
        peers, n = self.peers, self.n
        span = blocks[0].shape[0]
        length = n * span
        starts = [peers.source(step) * span for step in range(n)]
        index = jnp.concatenate([start + jnp.arange(span, dtype=jnp.int32) for start in starts])
        segments = jnp.concatenate(peers.spread(segment_ids), axis=1)[0]
        doc_start = jnp.sum((segments[None, :] < segments[:, None]).astype(jnp.int32), axis=1)
        self.cos_table, self.sin_table = rope_tables(index - doc_start)
        self.visible = (index[None, :] <= index[:, None]) & (
            segments[None, :] == segments[:, None]
        )
        self.scale = 1.0 / math.sqrt(HD)
        self.resid = jnp.concatenate(blocks).astype(F32)
        self.inv = inv_rms_of(self.resid)
        self.normed = (self.resid * self.inv * gain).astype(BF)
        projected = dot(self.normed, self.joint)[:, : self.cols] + self.bias_slice
        query_pre = projected[:, : self.q_cols].reshape(length, self.heads, HD)
        key_pre = projected[:, self.q_cols : self.q_cols + HD].reshape(length, 1, HD)
        self.values = projected[:, self.q_cols + HD : self.cols].astype(BF)
        self.query = rotate(query_pre, self.cos_table, self.sin_table).astype(BF)
        self.key = rotate(key_pre, self.cos_table, self.sin_table).astype(BF).reshape(length, HD)
        attended, self.log_total = attend(
            self.query, self.key, self.values, self.visible, self.scale
        )
        self.attended = attended.astype(BF)
        flat = self.attended.reshape(length, self.q_cols)
        mixed = add_up(peers.deliver(dot(flat, self.out_slice).astype(BF)))
        return blocks[0].astype(F32) + mixed

    def backward(self, mid_grad, gain, gain_two_term, filled, joint_grad, finish):
        peers, n, rows, dp_n = self.peers, self.n, self.rows, self.dp_n
        span = mid_grad.shape[0]
        blocks, filled = lax.optimization_barrier((peers.spread(mid_grad.astype(BF)), filled))
        filled = peers.deliver(filled)
        low = jnp.concatenate(blocks)
        length = low.shape[0]
        attended_grad = dot_t(low, self.out_slice).astype(BF).reshape(length, self.heads, HD)
        out_term = t_dot(self.attended.reshape(length, self.q_cols), low)
        query_grad, key_grad, value_grad = attend_back(
            self.query,
            self.key,
            self.values,
            self.visible,
            self.attended,
            attended_grad,
            self.log_total,
            self.scale,
        )
        query_grad = rotate(query_grad, self.cos_table, -self.sin_table).reshape(length, -1)
        key_grad = rotate(key_grad[:, None], self.cos_table, -self.sin_table).reshape(length, HD)
        proj_grad = jnp.concatenate([query_grad, key_grad, value_grad], axis=1)
        bias_term = jnp.sum(proj_grad, axis=0)
        low_grad = pad_to(proj_grad.astype(BF), 1, self.width)
        partial = dot_t(low_grad, self.joint).astype(BF)
        partial, filled = lax.optimization_barrier((partial, filled))
        normed_shares = peers.deliver(partial)
        gain_term = jnp.sum(partial.astype(F32) * (self.resid * self.inv), axis=0)
        qkv_term = t_dot(self.normed, low_grad)
        bias = jnp.zeros((dp_n * n * self.bias_rows,), F32)
        first = 0
        for start, size in self.places():
            bias = lax.dynamic_update_slice(bias, bias_term[first : first + size], (start,))
            first += size
        bias = pad_to(bias.reshape(dp_n * n, self.bias_rows), 1, self.bias_cols * rows)
        bias = bias.reshape(dp_n * n, self.bias_cols, rows).transpose(1, 0, 2)
        extra = jnp.concatenate(
            [gain_term[None], gain_two_term[None], bias.reshape(self.bias_cols, -1)], axis=0
        ).T
        extra = jnp.pad(extra, ((0, 0), (self.cols, self.width - self.cols - extra.shape[1])))
        joint = (qkv_term + extra).astype(BF).reshape(dp_n, n * rows, self.width)
        out_term = out_term.astype(BF).reshape(dp_n, self.extra_rows, self.width)
        pack, joint_grad, normed_shares = lax.optimization_barrier(
            (jnp.concatenate([joint, out_term], axis=1), joint_grad, normed_shares)
        )
        mine = lax.psum_scatter(pack, "dp", scatter_dimension=0, tiled=False)
        own = slice(0, span)
        normed_grad = add_up(normed_shares)
        input_grad = mid_grad + norm_back(normed_grad, self.resid[own], self.inv[own], gain)
        mine, input_grad, output, finished = lax.optimization_barrier(
            (mine, input_grad, *finish(filled, joint_grad))
        )
        moves = [((b % dp_n) * n + b // dp_n, b) for b in range(dp_n * n)]
        out_grad = lax.ppermute(
            mine[n * rows :].reshape(self.out_rows, self.out_cols), ALL, moves
        ).astype(F32)
        parts = lax.all_to_all(
            mine[: n * rows].reshape(n, rows, self.width), "ctx", 0, 0, tiled=True
        ).astype(F32)
        query = parts[:, :, : self.q_cols].transpose(1, 0, 2).reshape(rows, -1)
        both = parts[:, :, self.q_cols : self.cols].reshape(KV, self.share, rows, 2, HD)
        both = jnp.sum(both, axis=1).transpose(1, 2, 0, 3).reshape(rows, -1)
        extra = jnp.sum(parts[:, :, self.cols :], axis=0)
        bias_grad = extra[:, 2 : 2 + self.bias_cols].T.reshape(-1)[: self.bias_rows]
        return (
            input_grad,
            extra[:, 0],
            jnp.concatenate([query, both], axis=1),
            bias_grad,
            out_grad,
            extra[:, 1],
        ), output, finished


class RowSplit:
    def __init__(self, peers):
        self.peers = peers

    def gather(self, attn_gain, mlp_gain, qkv_weight, qkv_bias, out_weight):
        gain_one, gain_two, self.qkv, bias, self.out = (
            lax.all_gather(part, ALL, axis=0, tiled=True)
            for part in (attn_gain, mlp_gain, qkv_weight, qkv_bias, out_weight)
        )
        self.bias = bias.astype(F32)
        return gain_one.astype(F32), gain_two.astype(F32)

    def forward(self, blocks, segment_ids, gain):
        own = blocks[0]
        span = own.shape[0]
        width = KV * HD
        segments = segment_ids[0]
        all_segments = lax.all_gather(segment_ids, "ctx", axis=1, tiled=True)[0]
        length = all_segments.shape[0]
        query_index = self.peers.me * span + jnp.arange(span, dtype=jnp.int32)
        key_index = jnp.arange(length, dtype=jnp.int32)
        doc_start = jnp.sum((all_segments[None] < segments[:, None]).astype(jnp.int32), axis=1)
        self.cos_table, self.sin_table = rope_tables(query_index - doc_start)
        self.visible = (key_index[None, :] <= query_index[:, None]) & (
            all_segments[None, :] == segments[:, None]
        )
        self.scale = 1.0 / math.sqrt(HD)
        self.resid = own.astype(F32)
        self.inv = inv_rms_of(self.resid)
        self.normed = (self.resid * self.inv * gain).astype(BF)
        projected = dot(self.normed, self.qkv) + self.bias
        query_pre = projected[:, : H * HD].reshape(span, H, HD)
        key_pre = projected[:, H * HD : H * HD + width].reshape(span, KV, HD)
        values = projected[:, H * HD + width :].astype(BF)
        self.query = rotate(query_pre, self.cos_table, self.sin_table).astype(BF)
        key_rot = rotate(key_pre, self.cos_table, self.sin_table).astype(BF).reshape(span, width)
        self.key, self.values = (
            lax.all_gather(part, "ctx", axis=0, tiled=True).reshape(length, KV, HD)
            for part in (key_rot, values)
        )
        pieces = [
            attend(
                self.query[:, self.part(group)],
                self.key[:, group],
                self.values[:, group],
                self.visible,
                self.scale,
            )
            for group in range(KV)
        ]
        self.attended = jnp.concatenate([piece[0] for piece in pieces], axis=1).astype(BF)
        self.log_totals = [piece[1] for piece in pieces]
        return self.resid + dot(self.attended.reshape(span, -1), self.out)

    @staticmethod
    def part(group):
        return slice(group * (H // KV), (group + 1) * (H // KV))

    def backward(self, mid_grad, gain, gain_two_term, filled, joint_grad, finish):
        span = mid_grad.shape[0]
        low = mid_grad.astype(BF)
        attended_grad = dot_t(low, self.out).astype(BF).reshape(span, H, HD)
        grads = [
            attend_back(
                self.query[:, self.part(group)],
                self.key[:, group],
                self.values[:, group],
                self.visible,
                self.attended[:, self.part(group)],
                attended_grad[:, self.part(group)],
                self.log_totals[group],
                self.scale,
            )
            for group in range(KV)
        ]
        query_grad = jnp.concatenate([grad[0] for grad in grads], axis=1)
        key_grad, value_grad = (
            lax.psum_scatter(
                jnp.concatenate([grad[place] for grad in grads], axis=1).astype(BF),
                "ctx",
                scatter_dimension=0,
                tiled=True,
            ).astype(F32)
            for place in (1, 2)
        )
        query_grad = rotate(query_grad, self.cos_table, -self.sin_table).reshape(span, -1)
        key_grad = rotate(key_grad.reshape(span, KV, HD), self.cos_table, -self.sin_table)
        proj_grad = jnp.concatenate([query_grad, key_grad.reshape(span, -1), value_grad], axis=1)
        low_grad = proj_grad.astype(BF)
        normed_grad = dot_t(low_grad, self.qkv)
        input_grad = mid_grad + norm_back(normed_grad, self.resid, self.inv, gain)
        gain_term = jnp.sum(normed_grad * (self.resid * self.inv), axis=0)
        terms = (
            gain_term,
            t_dot(self.normed, low_grad).astype(BF),
            jnp.sum(proj_grad, axis=0),
            t_dot(self.attended.reshape(span, -1), low).astype(BF),
            gain_two_term,
        )
        grads = (input_grad,) + tuple(
            lax.psum_scatter(term, ALL, scatter_dimension=0, tiled=True).astype(F32)
            for term in terms
        )
        return grads, *finish(self.peers.deliver(filled), joint_grad)


def on_device(
    inputs,
    cotangent,
    segment_ids,
    attn_gain,
    qkv_weight,
    qkv_bias,
    out_weight,
    mlp_gain,
    gate_weight,
    up_weight,
    down_weight,
    *,
    dp_n,
    ctx_n,
):
    rows, hidden_width = gate_weight.shape
    n = ctx_n
    peers = Peers("ctx", n)
    if HeadSplit.fits(n, dp_n) and out_weight.shape[0] == rows:
        attention = HeadSplit(peers, dp_n, rows, qkv_bias.shape[0])
        blocks = peers.spread(inputs[0])
    else:
        attention = RowSplit(peers)
        blocks = [inputs[0]]
    gain_one, gain_two = attention.gather(attn_gain, mlp_gain, qkv_weight, qkv_bias, out_weight)

    unit = hidden_width // (dp_n * n)
    padded = round_up(unit, LANES // math.gcd(LANES, dp_n))
    wide = dp_n * padded

    def column_slices(weight):
        parts = pad_to(weight.reshape(rows, dp_n, n, unit), 3, padded)
        return parts.transpose(2, 0, 1, 3).reshape(n, rows, wide)

    def weight_columns(values):
        parts = values.reshape(n, rows, dp_n, padded)[..., :unit].transpose(1, 2, 0, 3)
        return parts.reshape(rows, hidden_width).astype(F32)

    joint = jnp.concatenate([column_slices(gate_weight), column_slices(up_weight)], axis=2)
    joint = peers.exchange(joint).reshape(n * rows, 2 * wide)
    gate_up = lax.all_gather(joint, "dp", axis=0, tiled=True)
    down = lax.all_gather(pad_to(down_weight, 0, padded), "dp", axis=0, tiled=True)

    resid_mid = attention.forward(blocks, segment_ids, gain_one)
    inv_two = inv_rms_of(resid_mid)
    normed_own = (resid_mid * inv_two * gain_two).astype(BF)
    blocks, gate_up, own_cotangent = lax.optimization_barrier(
        (peers.spread(normed_own), gate_up, cotangent[0])
    )
    normed = jnp.concatenate(blocks)
    grad_out = jnp.concatenate(peers.spread(own_cotangent))
    pre = dot(normed, gate_up)
    gate_pre = pre[:, :wide]
    up_pre = pre[:, wide:]
    sigmoid_gate = jax.nn.sigmoid(gate_pre)
    silu_gate = gate_pre * sigmoid_gate
    hidden = (silu_gate * up_pre).astype(BF)
    down_term = t_dot(hidden, grad_out).astype(BF)
    down_term, grad_out = lax.optimization_barrier((down_term, grad_out))
    down_grad = lax.psum_scatter(down_term, "dp", scatter_dimension=0, tiled=True)
    hidden_grad = dot_t(grad_out, down)
    gate_grad = (
        hidden_grad * up_pre * sigmoid_gate * (1.0 + gate_pre * (1.0 - sigmoid_gate))
    ).astype(BF)
    up_grad = (hidden_grad * silu_gate).astype(BF)
    pre_grad = jnp.concatenate([gate_grad, up_grad], axis=1)
    shares = peers.deliver(dot_t(pre_grad, gate_up).astype(BF))
    joint_term = t_dot(normed, pre_grad).astype(BF)
    shares, joint_term = lax.optimization_barrier((shares, joint_term))
    joint_term, down_grad = lax.optimization_barrier((joint_term, down_grad))
    joint_grad = lax.psum_scatter(joint_term, "dp", scatter_dimension=0, tiled=True)

    normed_two_grad = add_up(shares)
    gain_two_term = jnp.sum(normed_two_grad * (resid_mid * inv_two), axis=0)
    mid_grad = cotangent[0].astype(F32) + norm_back(normed_two_grad, resid_mid, inv_two, gain_two)

    def finish(output_shares, joint_grad):
        output = resid_mid + add_up(output_shares)
        parts = peers.exchange(joint_grad.reshape(n, rows, 2 * wide))
        grads = (weight_columns(parts[:, :, :wide]), weight_columns(parts[:, :, wide:]))
        return output.astype(BF), grads

    grads, output, (gate_weight_grad, up_weight_grad) = attention.backward(
        mid_grad, gain_one, gain_two_term, dot(hidden, down).astype(BF), joint_grad, finish
    )
    input_grad, attn_gain_grad, qkv_weight_grad, qkv_bias_grad, out_weight_grad, mlp_gain_grad = (
        grads
    )
    return (
        output[None],
        input_grad[None],
        attn_gain_grad,
        qkv_weight_grad,
        qkv_bias_grad,
        out_weight_grad,
        mlp_gain_grad,
        gate_weight_grad,
        up_weight_grad,
        down_grad[:unit].astype(F32),
    )


def solution(mesh):
    body = functools.partial(on_device, dp_n=mesh.shape["dp"], ctx_n=mesh.shape["ctx"])
    return jax.shard_map(
        body,
        mesh=mesh,
        in_specs=(
            P("dp", "ctx", None),
            P("dp", "ctx", None),
            P("dp", "ctx"),
            P(ALL),
            P(ALL, None),
            P(ALL),
            P(ALL, None),
            P(ALL),
            P(ALL, None),
            P(ALL, None),
            P(ALL, None),
        ),
        out_specs=(
            P("dp", "ctx", None),
            P("dp", "ctx", None),
            P(ALL),
            P(ALL, None),
            P(ALL),
            P(ALL, None),
            P(ALL),
            P(ALL, None),
            P(ALL, None),
            P(ALL, None),
        ),
        check_vma=False,
    )
```
